32 devices in a mesh: grp: 4 (over y, x), inner: 8 (over z, core).
Axes of the slice: x: 2, y: 2, z: 4, core: 2. Of those that a mesh axis runs over, the one named last changes fastest.
Arguments:
- tokens: bfloat16 [512, 8192], P('inner', 'grp'), may hold values from -170 to 170
- norm_gain: bfloat16 [8192], P('grp'), may hold values from 0.5 to 2
- gate_up_weight: bfloat16 [2, 8192, 28672], P(None, 'grp', 'inner'), may hold values from -0.0625 to 0.0625
- down_weight: bfloat16 [28672, 8192], P('inner', 'grp'), may hold values from -0.03125 to 0.03125
- student_in: bfloat16 [512, 1024], P('grp'), may hold values from -6 to 6
- student_proj: bfloat16 [1024, 8192], P(None, 'inner'), may hold values from -0.1875 to 0.1875
Outputs:
- teacher_out: bfloat16 [512, 8192], P('inner', 'grp')
- grad_student: float32 [512, 1024], P('grp')
- grad_proj: float32 [1024, 8192], P(None, 'inner')
The draws below stay inside these ranges and needn't reach their ends.
All inputs are finite; a program needn't handle non-finite values.
Results may differ from the reference program's by a relative error of at most 0.025.
Values may be sent and summed in bfloat16 or wider, within the bound.
No kernel may reach another device: no remote copies, remote signals or barrier semaphores. Data moves between devices by JAX's collectives and lax.ppermute only.
A program may use at most 128 MiB of HBM per device.

```python
import math
import jax
import jax.numpy as jnp
from jax import lax

D = 8192
FF = 28672
SD = 1024
ROWS = 512
N_GRP = 4


def draw_tokens(key, part):
    subkeys = jax.random.split(jax.random.fold_in(key, 11), 3)
    column_rise = 3.0 ** (jnp.arange(D, dtype=jnp.float32) / D) * jax.random.uniform(subkeys[1], (D,), jnp.float32, 0.7, 1.4)
    row_scale = jnp.exp(jax.random.uniform(subkeys[2], (ROWS, 1), jnp.float32, 0.0, math.log(10.0)))
    entries = jnp.clip(jax.random.normal(subkeys[0], (ROWS, D), jnp.float32), -4.0, 4.0)
    return (entries * column_rise[None, :] * row_scale).astype(jnp.bfloat16)


def steps_of(stream_key, extent, shards, smallest, top_value):
    factor_of, own = 1.0, jax.random.fold_in(stream_key, 6)
    for axis_at, shards_of in shards:
        heights = jnp.exp(jax.random.uniform(jax.random.fold_in(own, axis_at), (shards_of,), jnp.float32, smallest / len(shards), top_value / len(shards)))
        factor_of = factor_of * jnp.repeat(heights, extent[axis_at] // shards_of).reshape([-1 if axis == axis_at else 1 for axis in range(len(extent))])
    return factor_of


def noise(key, extent, width, reach, cuts=(), held_as=jnp.bfloat16):
    level = steps_of(key, extent, cuts, -0.22, 0.18) if cuts else 1.0
    values = jax.random.normal(key, extent, jnp.float32) * width * level
    return jnp.minimum(jnp.maximum(values, -reach), reach).astype(held_as)


def setup_inputs(seed: int = 0) -> dict:
    arg_keys = jax.random.split(jax.random.key(seed), 7)
    tokens = draw_tokens(jax.random.fold_in(arg_keys[6], 71), 0)
    norm_gain = jnp.clip(jnp.exp(math.log(2.0) - 1.3862944 * jax.random.uniform(arg_keys[1], (D,), jnp.float32) ** steps_of(arg_keys[1], (D,), ((0, 4),), -0.2, 0.2)), 0.5, 2.0).astype(jnp.bfloat16)
    gate_up_weight = noise(arg_keys[2], (2, D, FF), D ** -0.5, 0.0625, ((1, 4), (2, 8)))
    down_weight = noise(arg_keys[3], (FF, D), FF ** -0.5, 0.03125, ((0, 8), (1, 4)))
    student_in = noise(arg_keys[4], (ROWS, SD), 1.0, 6.0, ((0, 4),))
    student_proj = noise(arg_keys[5], (SD, D), SD ** -0.5, 0.1875, ((1, 8),))
    return dict(tokens=tokens, norm_gain=norm_gain, gate_up_weight=gate_up_weight, down_weight=down_weight, student_in=student_in, student_proj=student_proj)


def reference(tokens, norm_gain, gate_up_weight, down_weight, student_in, student_proj):
    values = tokens.astype(jnp.float32)
    mean_square = lax.optimization_barrier(jnp.mean(values * values, axis=1, keepdims=True))
    normed = (values * lax.rsqrt(mean_square + 1e-05) * norm_gain.astype(jnp.float32)[None, :]).astype(jnp.bfloat16)
    block_width = D // N_GRP
    gate_sum = jnp.zeros((ROWS, FF), jnp.float32)
    up_sum = jnp.zeros((ROWS, FF), jnp.float32)
    for block_index in range(N_GRP):
        lower = block_index * block_width
        piece = normed[:, lower:lower + block_width]
        gate_term = jnp.dot(piece, gate_up_weight[0, lower:lower + block_width, :], preferred_element_type=jnp.float32)
        up_term = jnp.dot(piece, gate_up_weight[1, lower:lower + block_width, :], preferred_element_type=jnp.float32)
        gate_sum = gate_sum + gate_term.astype(jnp.bfloat16).astype(jnp.float32)
        up_sum = up_sum + up_term.astype(jnp.bfloat16).astype(jnp.float32)
    hidden = (jax.nn.silu(gate_sum) * up_sum).astype(jnp.bfloat16)
    teacher_out = jnp.dot(hidden, down_weight, preferred_element_type=jnp.float32).astype(jnp.bfloat16)
    predicted = jnp.tanh(jnp.dot(student_in, student_proj, preferred_element_type=jnp.float32))
    mismatch = predicted - teacher_out.astype(jnp.float32)
    pre_grad = (mismatch * (1.0 - predicted * predicted)).astype(jnp.bfloat16)
    grad_student = jnp.dot(pre_grad, student_proj.T, preferred_element_type=jnp.float32)
    grad_proj = jnp.dot(student_in.T, pre_grad, preferred_element_type=jnp.float32)
    return (teacher_out, grad_student, grad_proj)
```

```python
import functools

import jax
import jax.numpy as jnp
from jax import lax
from jax.experimental import pallas as pl
from jax.experimental.pallas import tpu as pltpu
from jax.sharding import PartitionSpec as P

D = 8192
AXES = ("grp", "inner")
BF16 = jnp.bfloat16
F32 = jnp.float32
ROW_SHARES = (2, 2)
COL_CHUNKS = 2


def tile_of(extent, limit=256):
    tile = 128
    while tile * 2 <= limit and extent % (tile * 2) == 0:
        tile *= 2
    return tile if extent % tile == 0 else extent


def cost(flops, nbytes):
    return pl.CostEstimate(flops=int(flops), bytes_accessed=int(nbytes), transcendentals=0)


def scatter_list(order):
    blocks = [0]
    for bit in reversed(order):
        blocks = blocks + [block | (1 << bit) for block in blocks]
    return blocks


def gather_list(order):
    blocks = [0]
    for bit in order:
        blocks = blocks + [block ^ (1 << bit) for block in blocks]
    return blocks


def prepare_kernel(count, step, at_ref, *refs):
    pieces, gain_ref, out_ref = refs[:count], refs[count], refs[count + 1]
    gain = gain_ref[...].astype(F32)
    for offset in range(count):
        start = pl.multiple_of((at_ref[0] ^ offset) * step, step)
        out_ref[pl.ds(start, step), :] = (pieces[offset][...].astype(F32) * gain).astype(BF16)


def prepare(at, pieces, gain):
    count = len(pieces)
    step, width = pieces[0].shape
    whole = pl.BlockSpec(memory_space=pltpu.VMEM)
    return pl.pallas_call(
        functools.partial(prepare_kernel, count, step),
        out_shape=jax.ShapeDtypeStruct((count * step, width), BF16),
        in_specs=[pl.BlockSpec(memory_space=pltpu.SMEM)] + [whole] * (count + 1),
        out_specs=whole,
        cost_estimate=cost(count * step * width, 4 * count * step * width),
        name="prepare",
    )(at, *pieces, gain)


def up_kernel(block, lists, x_ref, w_ref, *outs):
    for k, blocks in enumerate(lists):
        total = jnp.dot(x_ref[...], w_ref[k], preferred_element_type=F32)
        half = len(blocks) // 2
        for slot, at in enumerate(blocks):
            ref = outs[2 * k + slot // half]
            row = (slot % half) * block
            ref[row : row + block, :] = total[at * block : (at + 1) * block, :].astype(BF16)


def up_product(x, weight, chunk, chunks, lists):
    rows, depth = x.shape
    groups = len(lists[0])
    block = rows // groups
    width = weight.shape[2] // chunks
    tile = tile_of(width)
    tiles = width // tile
    half = jax.ShapeDtypeStruct((rows // 2, width), BF16)
    return pl.pallas_call(
        functools.partial(up_kernel, block, lists),
        grid=(tiles,),
        out_shape=[half] * 4,
        in_specs=[
            pl.BlockSpec((rows, depth), lambda n: (0, 0)),
            pl.BlockSpec((2, depth, tile), lambda n: (0, 0, chunk * tiles + n)),
        ],
        out_specs=[pl.BlockSpec((rows // 2, tile), lambda n: (0, n))] * 4,
        cost_estimate=cost(4 * rows * depth * width, 4 * depth * width + 2 * rows * depth),
        name="up_product",
    )(x, weight)


def down_kernel(block, step, lists, first, last, at_ref, *refs):
    pieces, w_ref, refs = refs[:4], refs[4], refs[5:]
    if not first:
        before_ref, refs = refs[0], refs[1:]
    if last:
        keep_ref, send_ref, lhs_ref, total_ref = refs
    else:
        total_ref, lhs_ref = refs
    part = block // 2

    @pl.when(pl.program_id(0) == 0)
    def _():
        for stream, blocks in enumerate(lists):
            half = len(blocks) // 2
            for slot, at in enumerate(blocks):
                ref = pieces[2 * stream + slot // half]
                source = (slot % half) * part
                target = at * block + stream * part
                lhs_ref[target : target + part, :] = ref[source : source + part, :]

    total = jnp.dot(lhs_ref[...], w_ref[...], preferred_element_type=F32)
    if not first:
        total = total + before_ref[...]
    total_ref[...] = total
    if last:
        count = total.shape[0] // step
        for slot in range(count):
            start = pl.multiple_of((at_ref[0] ^ slot) * step, step)
            rows = total_ref[pl.ds(start, step), :]
            row = (slot // 2) * step
            if slot % 2 == 0:
                keep_ref[row : row + step, :] = rows
            else:
                send_ref[row : row + step, :] = rows.astype(BF16)


def down_product(at, pieces, weight, chunk, chunks, step, lists, before, last):
    groups = len(lists[0])
    part = pieces[0].shape[0] // (groups // 2)
    block = 2 * part
    rows = groups * block
    depth = weight.shape[0] // chunks
    width = weight.shape[1]
    tile = tile_of(width)
    whole = pl.BlockSpec(pieces[0].shape, lambda n: (0, 0))
    full = pl.BlockSpec((rows, tile), lambda n: (0, n))
    half = pl.BlockSpec((rows // 2, tile), lambda n: (0, n))
    in_specs = [pl.BlockSpec(memory_space=pltpu.SMEM)] + [whole] * 4
    in_specs.append(pl.BlockSpec((depth, tile), lambda n: (chunk, n)))
    operands = [at, *pieces, weight]
    if before is not None:
        in_specs.append(full)
        operands.append(before)
    scratch = [pltpu.VMEM((rows, depth), BF16)]
    if last:
        out_shape = [
            jax.ShapeDtypeStruct((rows // 2, width), F32),
            jax.ShapeDtypeStruct((rows // 2, width), BF16),
        ]
        out_specs = [half, half]
        scratch.append(pltpu.VMEM((rows, tile), F32))
    else:
        out_shape = jax.ShapeDtypeStruct((rows, width), F32)
        out_specs = full
    return pl.pallas_call(
        functools.partial(down_kernel, block, step, lists, before is None, last),
        grid=(width // tile,),
        out_shape=out_shape,
        in_specs=in_specs,
        out_specs=out_specs,
        scratch_shapes=scratch,
        cost_estimate=cost(2 * rows * depth * width, 2 * depth * width + 2 * rows * depth),
        name="down_product",
    )(*operands)


def place_kernel(count, step, cores, at_ref, *refs):
    pieces, out_ref = refs[:count], refs[count]
    for offset in range(count):
        source = at_ref[0] ^ offset
        slot = (source % cores) * (count // cores) + source // cores
        start = pl.multiple_of(slot * step, step)
        out_ref[pl.ds(start, step), :] = pieces[offset][...].astype(F32)


def place(at, pieces, cores):
    count = len(pieces)
    step, width = pieces[0].shape
    whole = pl.BlockSpec(memory_space=pltpu.VMEM)
    return pl.pallas_call(
        functools.partial(place_kernel, count, step, cores),
        out_shape=jax.ShapeDtypeStruct((count * step, width), F32),
        in_specs=[pl.BlockSpec(memory_space=pltpu.SMEM)] + [whole] * count,
        out_specs=whole,
        cost_estimate=cost(count * step * width, 6 * count * step * width),
        name="place",
    )(at, *pieces)


def shards(tokens, norm_gain, gate_up_weight, down_weight, student_in, student_proj):
    groups = lax.axis_size("grp")
    inner = lax.axis_size("inner")
    cores = inner // groups
    depth = inner // 2
    g = lax.axis_index("grp")
    i = lax.axis_index("inner")
    c = i % cores
    b = i // cores
    local_rows = tokens.shape[0]
    at_grp = (i ^ (cores * g)).astype(jnp.int32).reshape(1)
    at_inner = i.astype(jnp.int32).reshape(1)

    places = [(x, y) for x in range(groups) for y in range(inner)]

    def move(value, target):
        pairs = []
        for x, y in places:
            to_x, to_y = target(x, y)
            pairs.append((x * inner + y, to_x * inner + to_y))
        return lax.ppermute(value, AXES, pairs)

    def over_grp(value, mask):
        return move(value, lambda x, y: (x ^ mask, y))

    def over_inner(value, mask):
        return move(value, lambda x, y: (x, y ^ mask))

    def transpose(value):
        return move(value, lambda x, y: (y // cores, x * cores + y % cores))

    bits = list(range(groups.bit_length() - 1))
    orders = (bits, bits[::-1])
    scatter_lists = tuple(tuple(scatter_list(order)) for order in orders)
    gather_lists = tuple(tuple(gather_list(order)) for order in orders)

    def scatter(keep, send, order):
        block = keep.shape[0] * 2 // groups
        keep = keep.astype(F32)
        for stage, bit in enumerate(order):
            arrived = over_grp(send, 1 << bit)
            keep = keep + arrived.astype(F32)
            rows = keep.shape[0] // 2
            if rows >= block:
                keep, send = keep[:rows], keep[rows:].astype(BF16)
        return keep

    def gather(value, order):
        for bit in order[:-1]:
            value = jnp.concatenate([value, over_grp(value, 1 << bit)], axis=0)
        return value, over_grp(value, 1 << order[-1])

    share_total = sum(ROW_SHARES)
    steps = [local_rows * share // share_total for share in ROW_SHARES]
    starts = [sum(steps[:r]) for r in range(len(steps))]

    values = tokens.astype(F32)
    squares = jnp.sum(values * values, axis=1)[None, :]
    for bit in bits:
        squares = squares + over_grp(squares, 1 << bit)
    mine = transpose(squares)
    row_squares = [None] * cores
    others = [mine] + [over_inner(mine, offset) for offset in range(1, cores)]
    for core in range(cores):
        chosen = others[0]
        for offset in range(1, cores):
            chosen = jnp.where((c ^ core) == offset, others[offset], chosen)
        row_squares[core] = chosen[0]

    gain = norm_gain[None, :]

    def gather_rows(r):
        own = tokens[starts[r] : starts[r] + steps[r]]
        pieces = [None] * inner
        pieces[0] = own
        for far in range(1, depth):
            pieces[2 * far] = over_inner(own, 2 * far)
        for far in range(depth):
            pieces[2 * far + 1] = over_inner(pieces[2 * far], 1)
        return prepare(at_grp, pieces, gain)

    proj_other = over_inner(student_proj, 1)
    student_own = lax.dynamic_slice_in_dim(student_in, c * local_rows, local_rows, 0)
    student_other = lax.dynamic_slice_in_dim(
        student_in, (cores - 1 - c) * local_rows, local_rows, 0
    )
    student_pieces = []
    for order, value in zip(orders, (student_own, student_other)):
        student_pieces.extend(gather(value, order))
    student_all = jnp.concatenate(student_pieces, axis=0)
    predicted_own = jnp.tanh(jnp.dot(student_own, student_proj, preferred_element_type=F32))
    predicted_other = jnp.tanh(jnp.dot(student_own, proj_other, preferred_element_type=F32))

    teacher_parts = []
    target_parts = []
    for r, step in enumerate(steps):
        x = gather_rows(r)
        block = step * cores
        total = jnp.concatenate(
            [row_squares[core][starts[r] : starts[r] + step] for core in range(cores)]
        )
        inverse = lax.rsqrt(total / D + 1e-05)[:, None]
        before = None
        for chunk in range(COL_CHUNKS):
            gate_keep, gate_send, up_keep, up_send = up_product(
                x, gate_up_weight, chunk, COL_CHUNKS, scatter_lists
            )
            gate = scatter(gate_keep, gate_send, orders[0])
            up = scatter(up_keep, up_send, orders[1])
            pieces = []
            half = block // 2
            for stream, order in enumerate(orders):
                rows = slice(stream * half, (stream + 1) * half)
                hidden = jax.nn.silu(gate[rows] * inverse[rows]) * (up[rows] * inverse[rows])
                pieces.extend(gather(hidden.astype(BF16), order))
            last = chunk == COL_CHUNKS - 1
            before = down_product(
                at_grp, pieces, down_weight, chunk, COL_CHUNKS, step, gather_lists, before, last
            )
        keep, send = before
        keep = keep + over_inner(send, 1).astype(F32)
        result = keep[:step]
        for far in range(1, depth):
            piece = keep[far * step : (far + 1) * step].astype(BF16)
            result = result + over_inner(piece, 2 * far).astype(F32)
        result = result.astype(BF16)
        teacher_parts.append(result)
        target_parts.append(transpose(result))

    teacher_out = jnp.concatenate(teacher_parts, axis=0)
    target = jnp.concatenate(target_parts, axis=0)
    half = target.shape[1] // cores
    low, high = target[:, :half], target[:, half:]
    is_low = c == 0
    target_own = jnp.where(is_low, low, high).astype(F32)
    target_other = jnp.where(is_low, high, low).astype(F32)
    pre_own = ((predicted_own - target_own) * (1.0 - predicted_own * predicted_own)).astype(BF16)
    pre_other = (
        (predicted_other - target_other) * (1.0 - predicted_other * predicted_other)
    ).astype(BF16)
    pre_here = over_inner(pre_other, 1)

    contract = (((1,), (1,)), ((), ()))
    term = lax.dot_general(pre_own, student_proj, contract, preferred_element_type=F32)
    term = term + lax.dot_general(pre_other, proj_other, contract, preferred_element_type=F32)
    step = local_rows // depth
    total = lax.dynamic_slice_in_dim(term, b * step, step, 0)
    for far in range(1, depth):
        piece = lax.dynamic_slice_in_dim(term, (b ^ far) * step, step, 0).astype(BF16)
        total = total + over_inner(piece, 2 * far).astype(F32)
    total = total.astype(BF16)
    pieces = [None] * inner
    pieces[0] = total
    for far in range(1, depth):
        pieces[2 * far] = over_inner(total, 2 * far)
    for far in range(depth):
        pieces[2 * far + 1] = over_inner(pieces[2 * far], 1)
    grad_student = place(at_inner, pieces, cores)

    pre_pieces = []
    for order, value in zip(orders, (pre_own, pre_here)):
        pre_pieces.extend(gather(value, order))
    pre_all = jnp.concatenate(pre_pieces, axis=0)
    grad_proj = lax.dot_general(
        student_all, pre_all, (((0,), (0,)), ((), ())), preferred_element_type=F32
    )
    return (teacher_out, grad_student, grad_proj)


def solution(mesh):
    return jax.shard_map(
        shards,
        mesh=mesh,
        in_specs=(
            P("inner", "grp"),
            P("grp"),
            P(None, "grp", "inner"),
            P("inner", "grp"),
            P("grp", None),
            P(None, "inner"),
        ),
        out_specs=(P("inner", "grp"), P("grp", None), P(None, "inner")),
        check_vma=False,
    )
```

```python
import functools

import jax
import jax.numpy as jnp
from jax import lax
from jax.experimental import pallas as pl
from jax.experimental.pallas import tpu as pltpu
from jax.sharding import PartitionSpec as P


D = 8192
AXES = ("grp", "inner")
BF16 = jnp.bfloat16
F32 = jnp.float32
ROW_SHARES = (1, 2, 1)
COL_CHUNKS = 2
WEIGHT_PARTS = 2


def tile_of(extent, limit=1024):
    for tile in range(limit, 0, -128):
        if extent % tile == 0:
            return tile
    return extent


def cost(flops, nbytes):
    return pl.CostEstimate(flops=int(flops), bytes_accessed=int(nbytes), transcendentals=0)


def room(mebibytes):
    return pltpu.CompilerParams(vmem_limit_bytes=mebibytes << 20)


def whole_block(shape):
    return pl.BlockSpec(shape, lambda *at: (0,) * len(shape))


def scatter_list(order):
    blocks = [0]
    for bit in reversed(order):
        blocks = blocks + [block | (1 << bit) for block in blocks]
    return blocks


def gather_list(order):
    blocks = [0]
    for bit in order:
        blocks = blocks + [block ^ (1 << bit) for block in blocks]
    return blocks


def prepare_kernel(count, step, at_ref, *refs):
    pieces, gain_ref, out_ref = refs[:count], refs[count], refs[count + 1]
    gain = gain_ref[...].astype(F32)
    for offset in range(count):
        start = pl.multiple_of((at_ref[0] ^ offset) * step, step)
        out_ref[pl.ds(start, step), :] = (pieces[offset][...].astype(F32) * gain).astype(BF16)


def prepare(at, pieces, gain):
    count = len(pieces)
    step, width = pieces[0].shape
    return pl.pallas_call(
        functools.partial(prepare_kernel, count, step),
        grid=(1,),
        out_shape=jax.ShapeDtypeStruct((count * step, width), BF16),
        in_specs=[pl.BlockSpec(memory_space=pltpu.SMEM)]
        + [whole_block((step, width))] * count
        + [whole_block(gain.shape)],
        out_specs=whole_block((count * step, width)),
        cost_estimate=cost(count * step * width, 4 * count * step * width),
        name="prepare",
        compiler_params=room(8),
    )(at, *pieces, gain)


def up_kernel(block, blocks, parts, x_ref, *refs):
    w_refs, outs = refs[:parts], refs[parts:]
    part = w_refs[0].shape[0]
    total = 0.0
    for at, w_ref in enumerate(w_refs):
        total += jnp.dot(
            x_ref[:, at * part : (at + 1) * part], w_ref[...], preferred_element_type=F32
        )
    half = len(blocks) // 2
    for slot, at in enumerate(blocks):
        row = (slot % half) * block
        outs[slot // half][row : row + block, :] = total[at * block : (at + 1) * block, :].astype(
            BF16
        )


def up_product(x, weight, chunk, chunks, blocks):
    rows, depth = x.shape
    block = rows // len(blocks)
    width = weight.shape[2] // chunks
    tile = tile_of(width)
    tiles = width // tile
    half = jax.ShapeDtypeStruct((2, rows // 2, width), BF16)
    return pl.pallas_call(
        functools.partial(up_kernel, block, blocks, WEIGHT_PARTS),
        grid=(2, tiles),
        out_shape=[half] * 2,
        in_specs=[whole_block(x.shape)]
        + [
            pl.BlockSpec(
                (None, depth // WEIGHT_PARTS, tile),
                lambda k, n, at=at: (k, at, chunk * tiles + n),
            )
            for at in range(WEIGHT_PARTS)
        ],
        out_specs=[pl.BlockSpec((None, rows // 2, tile), lambda k, n: (k, 0, n))] * 2,
        cost_estimate=cost(4 * rows * depth * width, 4 * depth * width + 2 * rows * depth),
        name="up_product",
        compiler_params=room(44),
    )(x, *[weight] * WEIGHT_PARTS)


def add_kernel(keep_ref, arrived_ref, kept_ref, send_ref):
    rows = kept_ref.shape[0]
    total = keep_ref[...].astype(F32) + arrived_ref[...].astype(F32)
    kept_ref[...] = total[:rows]
    send_ref[...] = total[rows:].astype(BF16)


def add_halves(keep, arrived):
    _, rows, width = keep.shape
    whole = pl.BlockSpec((None, rows, width), lambda k: (k, 0, 0))
    half = pl.BlockSpec((None, rows // 2, width), lambda k: (k, 0, 0))
    return pl.pallas_call(
        add_kernel,
        grid=(2,),
        out_shape=[
            jax.ShapeDtypeStruct((2, rows // 2, width), F32),
            jax.ShapeDtypeStruct((2, rows // 2, width), BF16),
        ],
        in_specs=[whole] * 2,
        out_specs=[half] * 2,
        cost_estimate=cost(2 * rows * width, 14 * rows * width),
        name="add_halves",
        compiler_params=room(8),
    )(keep, arrived)


def squares_kernel(tokens_ref, out_ref):
    values = tokens_ref[...].astype(F32)
    total = jnp.sum(values * values, axis=1, keepdims=True)
    out_ref[...] = jnp.broadcast_to(total, out_ref.shape)


def row_squares(tokens):
    rows, width = tokens.shape
    return pl.pallas_call(
        squares_kernel,
        grid=(1,),
        out_shape=jax.ShapeDtypeStruct((rows, 128), F32),
        in_specs=[pl.BlockSpec((rows, width), lambda n: (0, 0))],
        out_specs=pl.BlockSpec((rows, 128), lambda n: (0, 0)),
        cost_estimate=cost(2 * rows * width, 2 * rows * width),
        name="row_squares",
        compiler_params=room(8),
    )(tokens)


def activate_kernel(cores, start, width, meta_ref, keep_ref, arrived_ref, *refs):
    squares, out_ref = refs[:cores], refs[cores]
    step = out_ref.shape[0] // cores
    for slot in range(cores):
        total = squares[0][start : start + step, :1]
        for offset in range(1, cores):
            other = squares[offset][start : start + step, :1]
            total = jnp.where((meta_ref[2] ^ slot) == offset, other, total)
        inverse = lax.rsqrt(total / width + 1e-05)
        rows = slice(slot * step, (slot + 1) * step)
        gate = (keep_ref[0, rows, :].astype(F32) + arrived_ref[0, rows, :].astype(F32)) * inverse
        up = (keep_ref[1, rows, :].astype(F32) + arrived_ref[1, rows, :].astype(F32)) * inverse
        out_ref[rows, :] = (jax.nn.silu(gate) * up).astype(BF16)


def activate(meta, keep, arrived, squares, start):
    _, rows, width = keep.shape
    tile = tile_of(width)
    both = pl.BlockSpec((2, rows, tile), lambda n: (0, 0, n))
    return pl.pallas_call(
        functools.partial(activate_kernel, len(squares), start, D),
        grid=(width // tile,),
        out_shape=jax.ShapeDtypeStruct((rows, width), BF16),
        in_specs=[pl.BlockSpec(memory_space=pltpu.SMEM), both, both]
        + [pl.BlockSpec(value.shape, lambda n: (0, 0)) for value in squares],
        out_specs=pl.BlockSpec((rows, tile), lambda n: (0, n)),
        cost_estimate=cost(10 * rows * width, 14 * rows * width),
        name="activate",
        compiler_params=room(8),
    )(meta, keep, arrived, *squares)


def join_kernel(near_ref, far_ref, out_ref):
    rows = near_ref.shape[0]
    out_ref[:rows, :] = near_ref[...]
    out_ref[rows:, :] = far_ref[...]


def join(near, far):
    rows, width = near.shape
    return pl.pallas_call(
        join_kernel,
        grid=(1,),
        out_shape=jax.ShapeDtypeStruct((2 * rows, width), near.dtype),
        in_specs=[pl.BlockSpec((rows, width), lambda n: (0, 0))] * 2,
        out_specs=pl.BlockSpec((2 * rows, width), lambda n: (0, 0)),
        cost_estimate=cost(rows * width, 8 * rows * width),
        name="join",
        compiler_params=room(8),
    )(near, far)


def down_kernel(block, step, blocks, parts, first, last, at_ref, near_ref, far_ref, *refs):
    w_refs, refs = refs[:parts], refs[parts:]
    if not first:
        before_ref, refs = refs[0], refs[1:]
    if last:
        keep_ref, send_ref, lhs_ref, total_ref = refs
    else:
        total_ref, lhs_ref = refs

    @pl.when(pl.program_id(0) == 0)
    def _():
        half = len(blocks) // 2
        for slot, at in enumerate(blocks):
            ref = far_ref if slot >= half else near_ref
            source = (slot % half) * block
            lhs_ref[at * block : (at + 1) * block, :] = ref[source : source + block, :]

    part = w_refs[0].shape[0]
    total = 0.0
    for at, w_ref in enumerate(w_refs):
        total += jnp.dot(
            lhs_ref[:, at * part : (at + 1) * part], w_ref[...], preferred_element_type=F32
        )
    if not first:
        total = total + before_ref[...]
    total_ref[...] = total
    if last:
        for slot in range(total.shape[0] // step):
            start = pl.multiple_of((at_ref[0] ^ slot) * step, step)
            rows = total_ref[pl.ds(start, step), :]
            row = (slot // 2) * step
            if slot % 2 == 0:
                keep_ref[row : row + step, :] = rows
            else:
                send_ref[row : row + step, :] = rows.astype(BF16)


def down_product(at, near, far, weight, chunk, chunks, step, blocks, before, last):
    rows = 2 * near.shape[0]
    depth = weight.shape[0] // chunks
    width = weight.shape[1]
    tile = tile_of(width)
    whole = pl.BlockSpec(near.shape, lambda n: (0, 0))
    full = pl.BlockSpec((rows, tile), lambda n: (0, n))
    half = pl.BlockSpec((rows // 2, tile), lambda n: (0, n))
    in_specs = [pl.BlockSpec(memory_space=pltpu.SMEM), whole, whole]
    parts = WEIGHT_PARTS
    for part in range(parts):
        in_specs.append(
            pl.BlockSpec((depth // parts, tile), lambda n, at=chunk * parts + part: (at, n))
        )
    operands = [at, near, far] + [weight] * parts
    if before is not None:
        in_specs.append(full)
        operands.append(before)
    scratch = [pltpu.VMEM((rows, depth), BF16)]
    if last:
        out_shape = [
            jax.ShapeDtypeStruct((rows // 2, width), F32),
            jax.ShapeDtypeStruct((rows // 2, width), BF16),
        ]
        out_specs = [half, half]
        scratch.append(pltpu.VMEM((rows, tile), F32))
    else:
        out_shape = jax.ShapeDtypeStruct((rows, width), F32)
        out_specs = full
    return pl.pallas_call(
        functools.partial(
            down_kernel, rows // len(blocks), step, blocks, parts, before is None, last
        ),
        grid=(width // tile,),
        out_shape=out_shape,
        in_specs=in_specs,
        out_specs=out_specs,
        scratch_shapes=scratch,
        cost_estimate=cost(2 * rows * depth * width, 2 * depth * width + 2 * rows * depth),
        name="down_product",
        compiler_params=room(14),
    )(*operands)


def split_kernel(count, keep_ref, arrived_ref, own_ref, *refs):
    step = own_ref.shape[0]
    own_ref[...] = keep_ref[:step, :] + arrived_ref[:step, :].astype(F32)
    for far in range(1, count):
        rows = slice(far * step, (far + 1) * step)
        refs[far - 1][...] = (keep_ref[rows, :] + arrived_ref[rows, :].astype(F32)).astype(BF16)


def split(keep, arrived, count):
    rows, width = keep.shape
    step = rows // count
    piece = jax.ShapeDtypeStruct((step, width), BF16)
    return pl.pallas_call(
        functools.partial(split_kernel, count),
        grid=(1,),
        out_shape=[jax.ShapeDtypeStruct((step, width), F32)] + [piece] * (count - 1),
        in_specs=[pl.BlockSpec((rows, width), lambda n: (0, 0))] * 2,
        out_specs=[pl.BlockSpec((step, width), lambda n: (0, 0))] * count,
        cost_estimate=cost(rows * width, 8 * rows * width),
        name="split",
        compiler_params=room(8),
    )(keep, arrived)


def take_kernel(meta_ref, rows_ref, out_ref):
    step = out_ref.shape[0]
    start = pl.multiple_of(meta_ref[2] * step, step)
    out_ref[...] = rows_ref[pl.ds(start, step), :]


def take_rows(meta, rows, step):
    return pl.pallas_call(
        take_kernel,
        grid=(1,),
        out_shape=jax.ShapeDtypeStruct((step, rows.shape[1]), rows.dtype),
        in_specs=[pl.BlockSpec(memory_space=pltpu.SMEM), whole_block(rows.shape)],
        out_specs=whole_block((step, rows.shape[1])),
        cost_estimate=cost(step, 4 * rows.size),
        name="take_rows",
        compiler_params=room(4),
    )(meta, rows)


def turn_kernel(near_ref, far_ref, out_ref):
    rows = near_ref.shape[0]
    out_ref[:, :rows] = near_ref[...].T
    out_ref[:, rows:] = far_ref[...].T


def turn(near, far):
    rows, width = near.shape
    return pl.pallas_call(
        turn_kernel,
        grid=(1,),
        out_shape=jax.ShapeDtypeStruct((width, 2 * rows), near.dtype),
        in_specs=[pl.BlockSpec((rows, width), lambda n: (0, 0))] * 2,
        out_specs=pl.BlockSpec((width, 2 * rows), lambda n: (0, 0)),
        cost_estimate=cost(rows * width, 8 * rows * width),
        name="turn",
        compiler_params=room(8),
    )(near, far)


def sum_kernel(own_ref, *refs):
    total = own_ref[...]
    for ref in refs[:-1]:
        total = total + ref[...].astype(F32)
    refs[-1][...] = total.astype(BF16)


def sum_rows(own, others):
    whole = pl.BlockSpec(own.shape, lambda n: (0, 0))
    return pl.pallas_call(
        sum_kernel,
        grid=(1,),
        out_shape=jax.ShapeDtypeStruct(own.shape, BF16),
        in_specs=[whole] * (1 + len(others)),
        out_specs=whole,
        cost_estimate=cost(own.size * len(others), 12 * own.size),
        name="sum_rows",
        compiler_params=room(8),
    )(own, *others)


def predict_kernel(rows_ref, proj_ref, other_ref, out_own_ref, out_other_ref):
    for weight, out in ((proj_ref, out_own_ref), (other_ref, out_other_ref)):
        out[...] = jnp.tanh(jnp.dot(rows_ref[...], weight[...], preferred_element_type=F32))


def predict(rows, proj, other):
    count, depth = rows.shape
    width = proj.shape[1]
    tile = tile_of(width, 512)
    weight = pl.BlockSpec((depth, tile), lambda n: (0, n))
    out = pl.BlockSpec((count, tile), lambda n: (0, n))
    return pl.pallas_call(
        predict_kernel,
        grid=(width // tile,),
        out_shape=[jax.ShapeDtypeStruct((count, width), F32)] * 2,
        in_specs=[pl.BlockSpec((count, depth), lambda n: (0, 0)), weight, weight],
        out_specs=[out, out],
        cost_estimate=cost(4 * count * depth * width, 4 * depth * width),
        name="predict",
        compiler_params=room(8),
    )(rows, proj, other)


def term_kernel(count, meta_ref, own_ref, other_ref, proj_ref, proj_other_ref, *refs):
    outs, total_ref = refs[:count], refs[count]
    contract = (((1,), (1,)), ((), ()))
    total = lax.dot_general(own_ref[...], proj_ref[...], contract, preferred_element_type=F32)
    total_ref[...] = total + lax.dot_general(
        other_ref[...], proj_other_ref[...], contract, preferred_element_type=F32
    )
    step = outs[0].shape[0]
    for far in range(count):
        start = pl.multiple_of((meta_ref[3] ^ far) * step, step)
        outs[far][...] = total_ref[pl.ds(start, step), :].astype(outs[far].dtype)


def student_term(meta, own, other, proj, proj_other, count):
    rows = own.shape[0]
    width = proj.shape[0]
    step = rows // count
    piece = jax.ShapeDtypeStruct((step, width), BF16)
    return pl.pallas_call(
        functools.partial(term_kernel, count),
        grid=(1,),
        out_shape=[jax.ShapeDtypeStruct((step, width), F32)] + [piece] * (count - 1),
        in_specs=[pl.BlockSpec(memory_space=pltpu.SMEM)]
        + [whole_block(own.shape)] * 2
        + [whole_block(proj.shape)] * 2,
        out_specs=[whole_block((step, width))] * count,
        scratch_shapes=[pltpu.VMEM((rows, width), F32)],
        cost_estimate=cost(4 * rows * proj.size, 4 * proj.size),
        name="student_term",
        compiler_params=room(14),
    )(meta, own, other, proj, proj_other)


def pre_kernel(starts, meta_ref, own_ref, other_ref, *refs):
    targets, out_refs = refs[: len(starts)], refs[len(starts) :]
    half = own_ref.shape[1]
    for offset, predicted_ref in enumerate((own_ref, other_ref)):
        column = pl.multiple_of((meta_ref[2] ^ offset) * half, half)
        for start, target_ref in zip(starts, targets):
            rows = slice(start, start + target_ref.shape[0])
            predicted = predicted_ref[rows, :]
            target = target_ref[:, pl.ds(column, half)].astype(F32)
            out_refs[offset][rows, :] = (
                (predicted - target) * (1.0 - predicted * predicted)
            ).astype(BF16)


def pre_gradient(meta, own, other, targets, starts):
    out = jax.ShapeDtypeStruct(own.shape, BF16)
    whole = pl.BlockSpec(own.shape, lambda n: (0, 0))
    return pl.pallas_call(
        functools.partial(pre_kernel, tuple(starts)),
        grid=(1,),
        out_shape=[out, out],
        in_specs=[pl.BlockSpec(memory_space=pltpu.SMEM), whole, whole]
        + [pl.BlockSpec(target.shape, lambda n: (0, 0)) for target in targets],
        out_specs=[whole, whole],
        cost_estimate=cost(8 * own.size, 16 * own.size),
        name="pre_gradient",
        compiler_params=room(8),
    )(meta, own, other, *targets)


def proj_kernel(rows, step, own_ref, other_ref, *refs):
    pieces, out_ref, rhs_ref = refs[: len(rows)], refs[len(rows)], refs[len(rows) + 1]
    for places, ref in zip(rows, pieces):
        for slot, at in enumerate(places):
            rhs_ref[at * step : (at + 1) * step, :] = ref[slot * step : (slot + 1) * step, :]
    half = own_ref.shape[1]
    out_ref[...] = jnp.dot(
        own_ref[...], rhs_ref[:half, :], preferred_element_type=F32
    ) + jnp.dot(other_ref[...], rhs_ref[half:, :], preferred_element_type=F32)


def proj_product(own, other, pieces, places, step):
    rows, depth = own.shape
    width = pieces[0].shape[1]
    tile = tile_of(width, 256)
    lhs = pl.BlockSpec((rows, depth), lambda n: (0, 0))
    return pl.pallas_call(
        functools.partial(proj_kernel, places, step),
        grid=(width // tile,),
        out_shape=jax.ShapeDtypeStruct((rows, width), F32),
        in_specs=[lhs, lhs]
        + [pl.BlockSpec((piece.shape[0], tile), lambda n: (0, n)) for piece in pieces],
        out_specs=pl.BlockSpec((rows, tile), lambda n: (0, n)),
        scratch_shapes=[pltpu.VMEM((2 * depth, tile), BF16)],
        cost_estimate=cost(4 * rows * depth * width, 4 * rows * width + 4 * rows * depth),
        name="proj_product",
        compiler_params=room(8),
    )(own, other, *pieces)


def place_kernel(count, step, cores, at_ref, *refs):
    pieces, out_ref = refs[:count], refs[count]
    for offset in range(count):
        source = at_ref[1] ^ offset
        slot = (source & (cores - 1)) * (count // cores) + (source >> (cores.bit_length() - 1))
        start = pl.multiple_of(slot * step, step)
        out_ref[pl.ds(start, step), :] = pieces[offset][...].astype(F32)


def place(at, pieces, cores):
    count = len(pieces)
    step, width = pieces[0].shape
    return pl.pallas_call(
        functools.partial(place_kernel, count, step, cores),
        grid=(1,),
        out_shape=jax.ShapeDtypeStruct((count * step, width), F32),
        in_specs=[pl.BlockSpec(memory_space=pltpu.SMEM)] + [whole_block((step, width))] * count,
        out_specs=whole_block((count * step, width)),
        cost_estimate=cost(count * step * width, 6 * count * step * width),
        name="place",
        compiler_params=room(4),
    )(at, *pieces)


def shards(tokens, norm_gain, gate_up_weight, down_weight, student_in, student_proj):
    groups = lax.axis_size("grp")
    inner = lax.axis_size("inner")
    cores = inner // groups
    depth = inner // 2
    g = lax.axis_index("grp")
    i = lax.axis_index("inner")
    c = i & (cores - 1)
    b = i >> (cores.bit_length() - 1)
    local_rows = tokens.shape[0]
    meta = jnp.stack([i ^ (cores * g), i, c, b]).astype(jnp.int32)
    meta, tokens = lax.optimization_barrier((meta, tokens))

    places = [(x, y) for x in range(groups) for y in range(inner)]

    def move(value, target):
        pairs = []
        for x, y in places:
            to_x, to_y = target(x, y)
            pairs.append((x * inner + y, to_x * inner + to_y))
        return lax.ppermute(value, AXES, pairs)

    def over_grp(value, mask):
        return move(value, lambda x, y: (x ^ mask, y))

    def over_inner(value, mask):
        return move(value, lambda x, y: (x, y ^ mask))

    def transpose(value):
        return move(value, lambda x, y: (y // cores, x * cores + y % cores))

    bits = list(range(groups.bit_length() - 1))
    orders = (bits, bits[::-1])

    def gather(value, order):
        for bit in order[:-1]:
            arrived = over_grp(value, 1 << bit)
            value = join(value, arrived)
        return value, over_grp(value, 1 << order[-1])

    share_total = sum(ROW_SHARES)
    steps = [local_rows * share // share_total for share in ROW_SHARES]
    starts = [sum(steps[:r]) for r in range(len(steps))]

    total = row_squares(tokens)
    for bit in bits:
        total = total + over_grp(total, 1 << bit)
    total = transpose(total)
    squares = [total] + [over_inner(total, offset) for offset in range(1, cores)]

    gain = norm_gain[None, :]

    def gather_rows(r):
        own = tokens[starts[r] : starts[r] + steps[r]]
        pieces = [None] * inner
        pieces[0] = own
        for far in range(1, depth):
            pieces[2 * far] = over_inner(own, 2 * far)
        for far in range(depth):
            pieces[2 * far + 1] = over_inner(pieces[2 * far], 1)
        return pieces

    proj_other = over_inner(student_proj, 1)
    student_own = take_rows(meta, student_in, local_rows)
    near, far_rows = gather(student_own, bits)
    student_cols = turn(near, far_rows)
    student_cols_other = over_inner(student_cols, 1)
    predicted_own, predicted_other = predict(student_own, student_proj, proj_other)

    teacher_parts = []
    target_parts = []
    for r, step in enumerate(steps):
        x = prepare(meta, gather_rows(r), gain)
        if r == len(steps) - 1:
            x, predicted_own, predicted_other = lax.optimization_barrier(
                (x, predicted_own, predicted_other)
            )
        before = None
        for chunk in range(COL_CHUNKS):
            u = r * COL_CHUNKS + chunk
            order = orders[u % 2]
            keep, send = up_product(
                x, gate_up_weight, chunk, COL_CHUNKS, scatter_list(order)
            )
            for stage, bit in enumerate(order):
                arrived = over_grp(send, 1 << bit)
                if stage < len(order) - 1:
                    keep, send = add_halves(keep, arrived)
            hidden = activate(meta, keep, arrived, squares, starts[r])
            near, far_rows = gather(hidden, order)
            last = chunk == COL_CHUNKS - 1
            before = down_product(
                meta,
                near,
                far_rows,
                down_weight,
                chunk,
                COL_CHUNKS,
                step,
                gather_list(order),
                before,
                last,
            )
        keep, send = before
        result, *sends = split(keep, over_inner(send, 1), depth)
        result = sum_rows(
            result,
            [over_inner(sends[far - 1], 2 * far) for far in range(1, depth)],
        )
        teacher_parts.append(result)
        target_parts.append(transpose(result))

    teacher_out = jnp.concatenate(teacher_parts, axis=0)
    pre_own, pre_other = pre_gradient(meta, predicted_own, predicted_other, target_parts, starts)
    pre_here = over_inner(pre_other, 1)

    own, *sends = student_term(meta, pre_own, pre_other, student_proj, proj_other, depth)
    total = sum_rows(own, [over_inner(sends[far - 1], 2 * far) for far in range(1, depth)])
    pieces = [None] * inner
    pieces[0] = total
    for far in range(1, depth):
        pieces[2 * far] = over_inner(total, 2 * far)
    for far in range(depth):
        pieces[2 * far + 1] = over_inner(pieces[2 * far], 1)
    grad_student = place(meta, pieces, cores)

    pre_pieces = []
    pre_places = []
    for half, value in enumerate((pre_own, pre_here)):
        pre_pieces.extend(gather(value, orders[half]))
        blocks = [half * groups + block for block in gather_list(orders[half])]
        pre_places.extend((blocks[: groups // 2], blocks[groups // 2 :]))
    grad_proj = proj_product(
        student_cols, student_cols_other, pre_pieces, pre_places, local_rows
    )
    return (teacher_out, grad_student, grad_proj)


def solution(mesh):
    return jax.shard_map(
        shards,
        mesh=mesh,
        in_specs=(
            P("inner", "grp"),
            P("grp"),
            P(None, "grp", "inner"),
            P("inner", "grp"),
            P("grp", None),
            P(None, "inner"),
        ),
        out_specs=(P("inner", "grp"), P("grp", None), P(None, "inner")),
        check_vma=False,
    )
```

```python
import functools

import jax
import jax.numpy as jnp
from jax import lax
from jax.experimental import pallas as pl
from jax.experimental.pallas import tpu as pltpu
from jax.sharding import PartitionSpec as P


D = 8192
AXES = ("grp", "inner")
BF16 = jnp.bfloat16
F32 = jnp.float32
ROW_SHARES = (1, 1)
COL_CHUNKS = 2
WEIGHT_PARTS = 2


def tile_of(extent, limit=1024):
    for tile in range(limit, 0, -128):
        if extent % tile == 0:
            return tile
    return extent


def cost(flops, nbytes):
    return pl.CostEstimate(flops=int(flops), bytes_accessed=int(nbytes), transcendentals=0)


def room(mebibytes):
    return pltpu.CompilerParams(vmem_limit_bytes=mebibytes << 20)


def whole_block(shape):
    return pl.BlockSpec(shape, lambda *at: (0,) * len(shape))


def scatter_list(order):
    blocks = [0]
    for bit in reversed(order):
        blocks = blocks + [block | (1 << bit) for block in blocks]
    return blocks


def gather_list(order):
    blocks = [0]
    for bit in order:
        blocks = blocks + [block ^ (1 << bit) for block in blocks]
    return blocks


def prepare_kernel(count, step, at_ref, *refs):
    pieces, gain_ref, out_ref = refs[:count], refs[count], refs[count + 1]
    gain = gain_ref[...].astype(F32)
    for offset in range(count):
        start = pl.multiple_of((at_ref[0] ^ offset) * step, step)
        out_ref[pl.ds(start, step), :] = (pieces[offset][...].astype(F32) * gain).astype(BF16)


def prepare(at, pieces, gain):
    count = len(pieces)
    step, width = pieces[0].shape
    return pl.pallas_call(
        functools.partial(prepare_kernel, count, step),
        grid=(1,),
        out_shape=jax.ShapeDtypeStruct((count * step, width), BF16),
        in_specs=[pl.BlockSpec(memory_space=pltpu.SMEM)]
        + [whole_block((step, width))] * count
        + [whole_block(gain.shape)],
        out_specs=whole_block((count * step, width)),
        cost_estimate=cost(count * step * width, 4 * count * step * width),
        name="prepare",
        compiler_params=room(8),
    )(at, *pieces, gain)


def up_kernel(block, blocks, parts, x_ref, *refs):
    w_refs, outs = refs[:parts], refs[parts:]
    part = w_refs[0].shape[0]
    total = 0.0
    for at, w_ref in enumerate(w_refs):
        total += jnp.dot(
            x_ref[:, at * part : (at + 1) * part], w_ref[...], preferred_element_type=F32
        )
    half = len(blocks) // 2
    for slot, at in enumerate(blocks):
        row = (slot % half) * block
        outs[slot // half][row : row + block, :] = total[at * block : (at + 1) * block, :].astype(
            BF16
        )


def up_product(x, weight, chunk, chunks, blocks):
    rows, depth = x.shape
    block = rows // len(blocks)
    width = weight.shape[2] // chunks
    tile = tile_of(width)
    tiles = width // tile
    half = jax.ShapeDtypeStruct((2, rows // 2, width), BF16)
    return pl.pallas_call(
        functools.partial(up_kernel, block, blocks, WEIGHT_PARTS),
        grid=(2, tiles),
        out_shape=[half] * 2,
        in_specs=[whole_block(x.shape)]
        + [
            pl.BlockSpec(
                (None, depth // WEIGHT_PARTS, tile),
                lambda k, n, at=at: (k, at, chunk * tiles + n),
            )
            for at in range(WEIGHT_PARTS)
        ],
        out_specs=[pl.BlockSpec((None, rows // 2, tile), lambda k, n: (k, 0, n))] * 2,
        cost_estimate=cost(4 * rows * depth * width, 4 * depth * width + 2 * rows * depth),
        name="up_product",
        compiler_params=room(44),
    )(x, *[weight] * WEIGHT_PARTS)


def add_kernel(keep_ref, arrived_ref, kept_ref, send_ref):
    rows = kept_ref.shape[0]
    total = keep_ref[...].astype(F32) + arrived_ref[...].astype(F32)
    kept_ref[...] = total[:rows]
    send_ref[...] = total[rows:].astype(BF16)


def add_halves(keep, arrived):
    _, rows, width = keep.shape
    whole = pl.BlockSpec((None, rows, width), lambda k: (k, 0, 0))
    half = pl.BlockSpec((None, rows // 2, width), lambda k: (k, 0, 0))
    return pl.pallas_call(
        add_kernel,
        grid=(2,),
        out_shape=[
            jax.ShapeDtypeStruct((2, rows // 2, width), F32),
            jax.ShapeDtypeStruct((2, rows // 2, width), BF16),
        ],
        in_specs=[whole] * 2,
        out_specs=[half] * 2,
        cost_estimate=cost(2 * rows * width, 14 * rows * width),
        name="add_halves",
        compiler_params=room(8),
    )(keep, arrived)


def squares_kernel(tokens_ref, out_ref):
    values = tokens_ref[...].astype(F32)
    total = jnp.sum(values * values, axis=1, keepdims=True)
    out_ref[...] = jnp.broadcast_to(total, out_ref.shape)


def row_squares(tokens):
    rows, width = tokens.shape
    return pl.pallas_call(
        squares_kernel,
        grid=(1,),
        out_shape=jax.ShapeDtypeStruct((rows, 128), F32),
        in_specs=[pl.BlockSpec((rows, width), lambda n: (0, 0))],
        out_specs=pl.BlockSpec((rows, 128), lambda n: (0, 0)),
        cost_estimate=cost(2 * rows * width, 2 * rows * width),
        name="row_squares",
        compiler_params=room(8),
    )(tokens)


def activate_kernel(cores, start, width, meta_ref, keep_ref, arrived_ref, *refs):
    squares, out_ref = refs[:cores], refs[cores]
    step = out_ref.shape[0] // cores
    for slot in range(cores):
        total = squares[0][start : start + step, :1]
        for offset in range(1, cores):
            other = squares[offset][start : start + step, :1]
            total = jnp.where((meta_ref[2] ^ slot) == offset, other, total)
        inverse = lax.rsqrt(total / width + 1e-05)
        rows = slice(slot * step, (slot + 1) * step)
        gate = (keep_ref[0, rows, :].astype(F32) + arrived_ref[0, rows, :].astype(F32)) * inverse
        up = (keep_ref[1, rows, :].astype(F32) + arrived_ref[1, rows, :].astype(F32)) * inverse
        out_ref[rows, :] = (jax.nn.silu(gate) * up).astype(BF16)


def activate(meta, keep, arrived, squares, start):
    _, rows, width = keep.shape
    tile = tile_of(width)
    both = pl.BlockSpec((2, rows, tile), lambda n: (0, 0, n))
    return pl.pallas_call(
        functools.partial(activate_kernel, len(squares), start, D),
        grid=(width // tile,),
        out_shape=jax.ShapeDtypeStruct((rows, width), BF16),
        in_specs=[pl.BlockSpec(memory_space=pltpu.SMEM), both, both]
        + [pl.BlockSpec(value.shape, lambda n: (0, 0)) for value in squares],
        out_specs=pl.BlockSpec((rows, tile), lambda n: (0, n)),
        cost_estimate=cost(10 * rows * width, 14 * rows * width),
        name="activate",
        compiler_params=room(8),
    )(meta, keep, arrived, *squares)


def join_kernel(near_ref, far_ref, out_ref):
    rows = near_ref.shape[0]
    out_ref[:rows, :] = near_ref[...]
    out_ref[rows:, :] = far_ref[...]


def join(near, far):
    rows, width = near.shape
    return pl.pallas_call(
        join_kernel,
        grid=(1,),
        out_shape=jax.ShapeDtypeStruct((2 * rows, width), near.dtype),
        in_specs=[pl.BlockSpec((rows, width), lambda n: (0, 0))] * 2,
        out_specs=pl.BlockSpec((2 * rows, width), lambda n: (0, 0)),
        cost_estimate=cost(rows * width, 8 * rows * width),
        name="join",
        compiler_params=room(8),
    )(near, far)


def down_kernel(block, step, blocks, parts, first, last, at_ref, near_ref, far_ref, *refs):
    w_refs, refs = refs[:parts], refs[parts:]
    if not first:
        before_ref, refs = refs[0], refs[1:]
    if last:
        keep_ref, send_ref, lhs_ref, total_ref = refs
    else:
        total_ref, lhs_ref = refs

    @pl.when(pl.program_id(0) == 0)
    def _():
        half = len(blocks) // 2
        for slot, at in enumerate(blocks):
            ref = far_ref if slot >= half else near_ref
            source = (slot % half) * block
            lhs_ref[at * block : (at + 1) * block, :] = ref[source : source + block, :]

    part = w_refs[0].shape[0]
    total = 0.0
    for at, w_ref in enumerate(w_refs):
        total += jnp.dot(
            lhs_ref[:, at * part : (at + 1) * part], w_ref[...], preferred_element_type=F32
        )
    if not first:
        total = total + before_ref[...]
    total_ref[...] = total
    if last:
        for slot in range(total.shape[0] // step):
            start = pl.multiple_of((at_ref[0] ^ slot) * step, step)
            rows = total_ref[pl.ds(start, step), :]
            row = (slot // 2) * step
            if slot % 2 == 0:
                keep_ref[row : row + step, :] = rows
            else:
                send_ref[row : row + step, :] = rows.astype(BF16)


def down_product(at, near, far, weight, chunk, chunks, step, blocks, before, last):
    rows = 2 * near.shape[0]
    depth = weight.shape[0] // chunks
    width = weight.shape[1]
    tile = tile_of(width)
    whole = pl.BlockSpec(near.shape, lambda n: (0, 0))
    full = pl.BlockSpec((rows, tile), lambda n: (0, n))
    half = pl.BlockSpec((rows // 2, tile), lambda n: (0, n))
    in_specs = [pl.BlockSpec(memory_space=pltpu.SMEM), whole, whole]
    parts = WEIGHT_PARTS
    for part in range(parts):
        in_specs.append(
            pl.BlockSpec((depth // parts, tile), lambda n, at=chunk * parts + part: (at, n))
        )
    operands = [at, near, far] + [weight] * parts
    if before is not None:
        in_specs.append(full)
        operands.append(before)
    scratch = [pltpu.VMEM((rows, depth), BF16)]
    if last:
        out_shape = [
            jax.ShapeDtypeStruct((rows // 2, width), F32),
            jax.ShapeDtypeStruct((rows // 2, width), BF16),
        ]
        out_specs = [half, half]
        scratch.append(pltpu.VMEM((rows, tile), F32))
    else:
        out_shape = jax.ShapeDtypeStruct((rows, width), F32)
        out_specs = full
    return pl.pallas_call(
        functools.partial(
            down_kernel, rows // len(blocks), step, blocks, parts, before is None, last
        ),
        grid=(width // tile,),
        out_shape=out_shape,
        in_specs=in_specs,
        out_specs=out_specs,
        scratch_shapes=scratch,
        cost_estimate=cost(2 * rows * depth * width, 2 * depth * width + 2 * rows * depth),
        name="down_product",
        compiler_params=room(14),
    )(*operands)


def split_kernel(count, keep_ref, arrived_ref, own_ref, *refs):
    step = own_ref.shape[0]
    own_ref[...] = keep_ref[:step, :] + arrived_ref[:step, :].astype(F32)
    for far in range(1, count):
        rows = slice(far * step, (far + 1) * step)
        refs[far - 1][...] = (keep_ref[rows, :] + arrived_ref[rows, :].astype(F32)).astype(BF16)


def split(keep, arrived, count):
    rows, width = keep.shape
    step = rows // count
    piece = jax.ShapeDtypeStruct((step, width), BF16)
    return pl.pallas_call(
        functools.partial(split_kernel, count),
        grid=(1,),
        out_shape=[jax.ShapeDtypeStruct((step, width), F32)] + [piece] * (count - 1),
        in_specs=[pl.BlockSpec((rows, width), lambda n: (0, 0))] * 2,
        out_specs=[pl.BlockSpec((step, width), lambda n: (0, 0))] * count,
        cost_estimate=cost(rows * width, 8 * rows * width),
        name="split",
        compiler_params=room(8),
    )(keep, arrived)


def take_kernel(meta_ref, rows_ref, out_ref):
    step = out_ref.shape[0]
    start = pl.multiple_of(meta_ref[2] * step, step)
    out_ref[...] = rows_ref[pl.ds(start, step), :]


def take_rows(meta, rows, step):
    return pl.pallas_call(
        take_kernel,
        grid=(1,),
        out_shape=jax.ShapeDtypeStruct((step, rows.shape[1]), rows.dtype),
        in_specs=[pl.BlockSpec(memory_space=pltpu.SMEM), whole_block(rows.shape)],
        out_specs=whole_block((step, rows.shape[1])),
        cost_estimate=cost(step, 4 * rows.size),
        name="take_rows",
        compiler_params=room(4),
    )(meta, rows)


def turn_kernel(near_ref, far_ref, out_ref):
    rows = near_ref.shape[0]
    out_ref[:, :rows] = near_ref[...].T
    out_ref[:, rows:] = far_ref[...].T


def turn(near, far):
    rows, width = near.shape
    return pl.pallas_call(
        turn_kernel,
        grid=(1,),
        out_shape=jax.ShapeDtypeStruct((width, 2 * rows), near.dtype),
        in_specs=[pl.BlockSpec((rows, width), lambda n: (0, 0))] * 2,
        out_specs=pl.BlockSpec((width, 2 * rows), lambda n: (0, 0)),
        cost_estimate=cost(rows * width, 8 * rows * width),
        name="turn",
        compiler_params=room(8),
    )(near, far)


def sum_kernel(own_ref, *refs):
    total = own_ref[...]
    for ref in refs[:-1]:
        total = total + ref[...].astype(F32)
    refs[-1][...] = total.astype(BF16)


def sum_rows(own, others):
    whole = pl.BlockSpec(own.shape, lambda n: (0, 0))
    return pl.pallas_call(
        sum_kernel,
        grid=(1,),
        out_shape=jax.ShapeDtypeStruct(own.shape, BF16),
        in_specs=[whole] * (1 + len(others)),
        out_specs=whole,
        cost_estimate=cost(own.size * len(others), 12 * own.size),
        name="sum_rows",
        compiler_params=room(8),
    )(own, *others)


def predict_kernel(rows_ref, proj_ref, other_ref, out_own_ref, out_other_ref):
    for weight, out in ((proj_ref, out_own_ref), (other_ref, out_other_ref)):
        out[...] = jnp.tanh(jnp.dot(rows_ref[...], weight[...], preferred_element_type=F32))


def predict(rows, proj, other):
    count, depth = rows.shape
    width = proj.shape[1]
    tile = tile_of(width, 512)
    weight = pl.BlockSpec((depth, tile), lambda n: (0, n))
    out = pl.BlockSpec((count, tile), lambda n: (0, n))
    return pl.pallas_call(
        predict_kernel,
        grid=(width // tile,),
        out_shape=[jax.ShapeDtypeStruct((count, width), F32)] * 2,
        in_specs=[pl.BlockSpec((count, depth), lambda n: (0, 0)), weight, weight],
        out_specs=[out, out],
        cost_estimate=cost(4 * count * depth * width, 4 * depth * width),
        name="predict",
        compiler_params=room(8),
    )(rows, proj, other)


def term_kernel(count, meta_ref, own_ref, other_ref, proj_ref, proj_other_ref, *refs):
    outs, total_ref = refs[:count], refs[count]
    contract = (((1,), (1,)), ((), ()))
    total = lax.dot_general(own_ref[...], proj_ref[...], contract, preferred_element_type=F32)
    total_ref[...] = total + lax.dot_general(
        other_ref[...], proj_other_ref[...], contract, preferred_element_type=F32
    )
    step = outs[0].shape[0]
    for far in range(count):
        start = pl.multiple_of((meta_ref[3] ^ far) * step, step)
        outs[far][...] = total_ref[pl.ds(start, step), :].astype(outs[far].dtype)


def student_term(meta, own, other, proj, proj_other, count):
    rows = own.shape[0]
    width = proj.shape[0]
    step = rows // count
    piece = jax.ShapeDtypeStruct((step, width), BF16)
    return pl.pallas_call(
        functools.partial(term_kernel, count),
        grid=(1,),
        out_shape=[jax.ShapeDtypeStruct((step, width), F32)] + [piece] * (count - 1),
        in_specs=[pl.BlockSpec(memory_space=pltpu.SMEM)]
        + [whole_block(own.shape)] * 2
        + [whole_block(proj.shape)] * 2,
        out_specs=[whole_block((step, width))] * count,
        scratch_shapes=[pltpu.VMEM((rows, width), F32)],
        cost_estimate=cost(4 * rows * proj.size, 4 * proj.size),
        name="student_term",
        compiler_params=room(14),
    )(meta, own, other, proj, proj_other)


def pre_kernel(starts, meta_ref, own_ref, other_ref, *refs):
    targets, out_refs = refs[: len(starts)], refs[len(starts) :]
    half = own_ref.shape[1]
    for offset, predicted_ref in enumerate((own_ref, other_ref)):
        column = pl.multiple_of((meta_ref[2] ^ offset) * half, half)
        for start, target_ref in zip(starts, targets):
            rows = slice(start, start + target_ref.shape[0])
            predicted = predicted_ref[rows, :]
            target = target_ref[:, pl.ds(column, half)].astype(F32)
            out_refs[offset][rows, :] = (
                (predicted - target) * (1.0 - predicted * predicted)
            ).astype(BF16)


def pre_gradient(meta, own, other, targets, starts):
    out = jax.ShapeDtypeStruct(own.shape, BF16)
    whole = pl.BlockSpec(own.shape, lambda n: (0, 0))
    return pl.pallas_call(
        functools.partial(pre_kernel, tuple(starts)),
        grid=(1,),
        out_shape=[out, out],
        in_specs=[pl.BlockSpec(memory_space=pltpu.SMEM), whole, whole]
        + [pl.BlockSpec(target.shape, lambda n: (0, 0)) for target in targets],
        out_specs=[whole, whole],
        cost_estimate=cost(8 * own.size, 16 * own.size),
        name="pre_gradient",
        compiler_params=room(8),
    )(meta, own, other, *targets)


def proj_kernel(rows, step, own_ref, other_ref, *refs):
    pieces, out_ref, rhs_ref = refs[: len(rows)], refs[len(rows)], refs[len(rows) + 1]
    for places, ref in zip(rows, pieces):
        for slot, at in enumerate(places):
            rhs_ref[at * step : (at + 1) * step, :] = ref[slot * step : (slot + 1) * step, :]
    half = own_ref.shape[1]
    out_ref[...] = jnp.dot(
        own_ref[...], rhs_ref[:half, :], preferred_element_type=F32
    ) + jnp.dot(other_ref[...], rhs_ref[half:, :], preferred_element_type=F32)


def proj_product(own, other, pieces, places, step):
    rows, depth = own.shape
    width = pieces[0].shape[1]
    tile = tile_of(width, 256)
    lhs = pl.BlockSpec((rows, depth), lambda n: (0, 0))
    return pl.pallas_call(
        functools.partial(proj_kernel, places, step),
        grid=(width // tile,),
        out_shape=jax.ShapeDtypeStruct((rows, width), F32),
        in_specs=[lhs, lhs]
        + [pl.BlockSpec((piece.shape[0], tile), lambda n: (0, n)) for piece in pieces],
        out_specs=pl.BlockSpec((rows, tile), lambda n: (0, n)),
        scratch_shapes=[pltpu.VMEM((2 * depth, tile), BF16)],
        cost_estimate=cost(4 * rows * depth * width, 4 * rows * width + 4 * rows * depth),
        name="proj_product",
        compiler_params=room(8),
    )(own, other, *pieces)


def place_kernel(count, step, cores, at_ref, *refs):
    pieces, out_ref = refs[:count], refs[count]
    for offset in range(count):
        source = at_ref[1] ^ offset
        slot = (source & (cores - 1)) * (count // cores) + (source >> (cores.bit_length() - 1))
        start = pl.multiple_of(slot * step, step)
        out_ref[pl.ds(start, step), :] = pieces[offset][...].astype(F32)


def place(at, pieces, cores):
    count = len(pieces)
    step, width = pieces[0].shape
    return pl.pallas_call(
        functools.partial(place_kernel, count, step, cores),
        grid=(1,),
        out_shape=jax.ShapeDtypeStruct((count * step, width), F32),
        in_specs=[pl.BlockSpec(memory_space=pltpu.SMEM)] + [whole_block((step, width))] * count,
        out_specs=whole_block((count * step, width)),
        cost_estimate=cost(count * step * width, 6 * count * step * width),
        name="place",
        compiler_params=room(4),
    )(at, *pieces)


def shards(tokens, norm_gain, gate_up_weight, down_weight, student_in, student_proj):
    groups = lax.axis_size("grp")
    inner = lax.axis_size("inner")
    cores = inner // groups
    depth = inner // 2
    g = lax.axis_index("grp")
    i = lax.axis_index("inner")
    c = i & (cores - 1)
    b = i >> (cores.bit_length() - 1)
    local_rows = tokens.shape[0]
    meta = jnp.stack([i ^ (cores * g), i, c, b]).astype(jnp.int32)
    meta, tokens = lax.optimization_barrier((meta, tokens))

    places = [(x, y) for x in range(groups) for y in range(inner)]

    def move(value, target):
        pairs = []
        for x, y in places:
            to_x, to_y = target(x, y)
            pairs.append((x * inner + y, to_x * inner + to_y))
        return lax.ppermute(value, AXES, pairs)

    def over_grp(value, mask):
        return move(value, lambda x, y: (x ^ mask, y))

    def over_inner(value, mask):
        return move(value, lambda x, y: (x, y ^ mask))

    def transpose(value):
        return move(value, lambda x, y: (y // cores, x * cores + y % cores))

    bits = list(range(groups.bit_length() - 1))
    orders = (bits, bits[::-1])

    def gather(value, order):
        for bit in order[:-1]:
            arrived = over_grp(value, 1 << bit)
            value = join(value, arrived)
        return value, over_grp(value, 1 << order[-1])

    share_total = sum(ROW_SHARES)
    steps = [local_rows * share // share_total for share in ROW_SHARES]
    starts = [sum(steps[:r]) for r in range(len(steps))]

    total = row_squares(tokens)
    for bit in bits:
        total = total + over_grp(total, 1 << bit)
    total = transpose(total)
    squares = [total] + [over_inner(total, offset) for offset in range(1, cores)]

    gain = norm_gain[None, :]

    def gather_rows(r):
        own = tokens[starts[r] : starts[r] + steps[r]]
        pieces = [None] * inner
        pieces[0] = own
        for far in range(1, depth):
            pieces[2 * far] = over_inner(own, 2 * far)
        for far in range(depth):
            pieces[2 * far + 1] = over_inner(pieces[2 * far], 1)
        return pieces

    proj_other = over_inner(student_proj, 1)
    student_own = take_rows(meta, student_in, local_rows)
    near, far_rows = gather(student_own, bits)
    student_cols = turn(near, far_rows)
    student_cols_other = over_inner(student_cols, 1)
    predicted_own, predicted_other = predict(student_own, student_proj, proj_other)

    teacher_parts = []
    target_parts = []
    for r, step in enumerate(steps):
        x = prepare(meta, gather_rows(r), gain)
        before = None
        for chunk in range(COL_CHUNKS):
            u = r * COL_CHUNKS + chunk
            order = orders[u % 2]
            keep, send = up_product(
                x, gate_up_weight, chunk, COL_CHUNKS, scatter_list(order)
            )
            for stage, bit in enumerate(order):
                arrived = over_grp(send, 1 << bit)
                if stage < len(order) - 1:
                    keep, send = add_halves(keep, arrived)
            hidden = activate(meta, keep, arrived, squares, starts[r])
            near, far_rows = gather(hidden, order)
            last = chunk == COL_CHUNKS - 1
            before = down_product(
                meta,
                near,
                far_rows,
                down_weight,
                chunk,
                COL_CHUNKS,
                step,
                gather_list(order),
                before,
                last,
            )
        keep, send = before
        result, *sends = split(keep, over_inner(send, 1), depth)
        result = sum_rows(
            result,
            [over_inner(sends[far - 1], 2 * far) for far in range(1, depth)],
        )
        teacher_parts.append(result)
        target_parts.append(transpose(result))

    teacher_out = jnp.concatenate(teacher_parts, axis=0)
    pre_own, pre_other = pre_gradient(meta, predicted_own, predicted_other, target_parts, starts)
    pre_here = over_inner(pre_other, 1)

    own, *sends = student_term(meta, pre_own, pre_other, student_proj, proj_other, depth)
    total = sum_rows(own, [over_inner(sends[far - 1], 2 * far) for far in range(1, depth)])
    pieces = [None] * inner
    pieces[0] = total
    for far in range(1, depth):
        pieces[2 * far] = over_inner(total, 2 * far)
    for far in range(depth):
        pieces[2 * far + 1] = over_inner(pieces[2 * far], 1)
    grad_student = place(meta, pieces, cores)

    pre_pieces = []
    pre_places = []
    for half, value in enumerate((pre_own, pre_here)):
        pre_pieces.extend(gather(value, orders[half]))
        blocks = [half * groups + block for block in gather_list(orders[half])]
        pre_places.extend((blocks[: groups // 2], blocks[groups // 2 :]))
    grad_proj = proj_product(student_cols, student_cols_other, pre_pieces, pre_places, local_rows)
    return (teacher_out, grad_student, grad_proj)


def solution(mesh):
    return jax.shard_map(
        shards,
        mesh=mesh,
        in_specs=(
            P("inner", "grp"),
            P("grp"),
            P(None, "grp", "inner"),
            P("inner", "grp"),
            P("grp", None),
            P(None, "inner"),
        ),
        out_specs=(P("inner", "grp"), P("grp", None), P(None, "inner")),
        check_vma=False,
    )
```

```python
import functools

import jax
import jax.numpy as jnp
from jax import lax
from jax.experimental import pallas as pl
from jax.experimental.pallas import tpu as pltpu
from jax.sharding import PartitionSpec as P


D = 8192
AXES = ("grp", "inner")
BF16 = jnp.bfloat16
F32 = jnp.float32
ROW_SHARES = (1, 1)
COL_CHUNKS = 2
WEIGHT_PARTS = 2


def tile_of(extent, limit=1024):
    for tile in range(limit, 0, -128):
        if extent % tile == 0:
            return tile
    return extent


def cost(flops, nbytes):
    return pl.CostEstimate(flops=int(flops), bytes_accessed=int(nbytes), transcendentals=0)


def room(mebibytes):
    return pltpu.CompilerParams(vmem_limit_bytes=mebibytes << 20)


def whole_block(shape):
    return pl.BlockSpec(shape, lambda *at: (0,) * len(shape))


def scatter_list(order):
    blocks = [0]
    for bit in reversed(order):
        blocks = blocks + [block | (1 << bit) for block in blocks]
    return blocks


def gather_list(order):
    blocks = [0]
    for bit in order:
        blocks = blocks + [block ^ (1 << bit) for block in blocks]
    return blocks


def prepare_kernel(count, step, at_ref, *refs):
    pieces, gain_ref, out_ref, squares_ref = refs[:count], *refs[count:]
    gain = gain_ref[...].astype(F32)
    for offset in range(count):
        start = pl.multiple_of((at_ref[0] ^ offset) * step, step)
        values = pieces[offset][...].astype(F32)
        out_ref[pl.ds(start, step), :] = (values * gain).astype(BF16)
        total = jnp.sum(values * values, axis=1, keepdims=True)
        squares_ref[pl.ds(start, step), :] = jnp.broadcast_to(total, (step, 128))


def prepare(at, pieces, gain):
    count = len(pieces)
    step, width = pieces[0].shape
    return pl.pallas_call(
        functools.partial(prepare_kernel, count, step),
        grid=(1,),
        out_shape=[
            jax.ShapeDtypeStruct((count * step, width), BF16),
            jax.ShapeDtypeStruct((count * step, 128), F32),
        ],
        in_specs=[pl.BlockSpec(memory_space=pltpu.SMEM)]
        + [whole_block((step, width))] * count
        + [whole_block(gain.shape)],
        out_specs=[whole_block((count * step, width)), whole_block((count * step, 128))],
        cost_estimate=cost(3 * count * step * width, 4 * count * step * width),
        name="prepare",
        compiler_params=room(8),
    )(at, *pieces, gain)


def up_kernel(block, blocks, start, tile, x_ref, source_ref, keep_ref, send_ref, w_ref, sems):
    tiles = w_ref.shape[2] // tile
    half = len(blocks) // 2

    def copy(k, n):
        column = pl.multiple_of(n * tile, tile)
        return pltpu.make_async_copy(
            source_ref.at[k, :, pl.ds(start + column, tile)],
            w_ref.at[k, :, pl.ds(column, tile)],
            sems.at[k, n],
        )

    for k in range(2):
        for n in range(tiles):
            copy(k, n).start()
    for k in range(2):

        @pl.loop(0, tiles)
        def _(n):
            copy(k, n).wait()
            columns = pl.ds(pl.multiple_of(n * tile, tile), tile)
            total = jnp.dot(x_ref[...], w_ref[k, :, columns], preferred_element_type=F32)
            for slot, at in enumerate(blocks):
                ref = send_ref if slot >= half else keep_ref
                row = (slot % half) * block
                ref[k, row : row + block, columns] = total[
                    at * block : (at + 1) * block, :
                ].astype(BF16)


def up_product(x, weight, chunk, chunks, blocks):
    rows, depth = x.shape
    width = weight.shape[2] // chunks
    tile = tile_of(width, 256)
    half = jax.ShapeDtypeStruct((2, rows // 2, width), BF16)
    return pl.pallas_call(
        functools.partial(up_kernel, rows // len(blocks), blocks, chunk * width, tile),
        grid=(1,),
        out_shape=[half] * 2,
        in_specs=[whole_block(x.shape), pl.BlockSpec(memory_space=pltpu.HBM)],
        out_specs=[whole_block(half.shape)] * 2,
        scratch_shapes=[
            pltpu.VMEM((2, depth, width), BF16),
            pltpu.SemaphoreType.DMA((2, width // tile)),
        ],
        cost_estimate=cost(4 * rows * depth * width, 4 * depth * width + 2 * rows * depth),
        name="up_product",
        compiler_params=room(32),
    )(x, weight)


def add_kernel(keep_ref, arrived_ref, kept_ref, send_ref):
    rows = kept_ref.shape[0]
    total = keep_ref[...].astype(F32) + arrived_ref[...].astype(F32)
    kept_ref[...] = total[:rows]
    send_ref[...] = total[rows:].astype(BF16)


def add_halves(keep, arrived):
    _, rows, width = keep.shape
    whole = pl.BlockSpec((None, rows, width), lambda k: (k, 0, 0))
    half = pl.BlockSpec((None, rows // 2, width), lambda k: (k, 0, 0))
    return pl.pallas_call(
        add_kernel,
        grid=(2,),
        out_shape=[
            jax.ShapeDtypeStruct((2, rows // 2, width), F32),
            jax.ShapeDtypeStruct((2, rows // 2, width), BF16),
        ],
        in_specs=[whole] * 2,
        out_specs=[half] * 2,
        cost_estimate=cost(2 * rows * width, 14 * rows * width),
        name="add_halves",
        compiler_params=room(8),
    )(keep, arrived)


def activate_kernel(depth, keep_ref, arrived_ref, squares_ref, out_ref):
    inverse = lax.rsqrt(squares_ref[:, :1] / depth + 1e-05)
    gate = (keep_ref[0].astype(F32) + arrived_ref[0].astype(F32)) * inverse
    up = (keep_ref[1].astype(F32) + arrived_ref[1].astype(F32)) * inverse
    out_ref[...] = (jax.nn.silu(gate) * up).astype(BF16)


def activate(keep, arrived, squares):
    _, rows, width = keep.shape
    tile = tile_of(width)
    both = pl.BlockSpec((2, rows, tile), lambda n: (0, 0, n))
    return pl.pallas_call(
        functools.partial(activate_kernel, D),
        grid=(width // tile,),
        out_shape=jax.ShapeDtypeStruct((rows, width), BF16),
        in_specs=[both, both, whole_block(squares.shape)],
        out_specs=pl.BlockSpec((rows, tile), lambda n: (0, n)),
        cost_estimate=cost(10 * rows * width, 14 * rows * width),
        name="activate",
        compiler_params=room(8),
    )(keep, arrived, squares)


def join_kernel(near_ref, far_ref, out_ref):
    rows = near_ref.shape[0]
    out_ref[:rows, :] = near_ref[...]
    out_ref[rows:, :] = far_ref[...]


def join(near, far):
    rows, width = near.shape
    return pl.pallas_call(
        join_kernel,
        grid=(1,),
        out_shape=jax.ShapeDtypeStruct((2 * rows, width), near.dtype),
        in_specs=[pl.BlockSpec((rows, width), lambda n: (0, 0))] * 2,
        out_specs=pl.BlockSpec((2 * rows, width), lambda n: (0, 0)),
        cost_estimate=cost(rows * width, 8 * rows * width),
        name="join",
        compiler_params=room(8),
    )(near, far)


def down_kernel(block, step, blocks, parts, first, last, at_ref, near_ref, far_ref, *refs):
    w_refs, refs = refs[:parts], refs[parts:]
    if not first:
        before_ref, refs = refs[0], refs[1:]
    if last:
        keep_ref, send_ref, lhs_ref, total_ref = refs
    else:
        total_ref, lhs_ref = refs

    @pl.when(pl.program_id(0) == 0)
    def _():
        half = len(blocks) // 2
        for slot, at in enumerate(blocks):
            ref = far_ref if slot >= half else near_ref
            source = (slot % half) * block
            lhs_ref[at * block : (at + 1) * block, :] = ref[source : source + block, :]

    part = w_refs[0].shape[0]
    total = 0.0
    for at, w_ref in enumerate(w_refs):
        total += jnp.dot(
            lhs_ref[:, at * part : (at + 1) * part], w_ref[...], preferred_element_type=F32
        )
    if not first:
        total = total + before_ref[...]
    total_ref[...] = total
    if last:
        for slot in range(total.shape[0] // step):
            start = pl.multiple_of((at_ref[0] ^ slot) * step, step)
            rows = total_ref[pl.ds(start, step), :]
            row = (slot // 2) * step
            if slot % 2 == 0:
                keep_ref[row : row + step, :] = rows
            else:
                send_ref[row : row + step, :] = rows.astype(BF16)


def down_product(at, near, far, weight, chunk, chunks, step, blocks, before, last):
    rows = 2 * near.shape[0]
    depth = weight.shape[0] // chunks
    width = weight.shape[1]
    tile = tile_of(width)
    whole = pl.BlockSpec(near.shape, lambda n: (0, 0))
    full = pl.BlockSpec((rows, tile), lambda n: (0, n))
    half = pl.BlockSpec((rows // 2, tile), lambda n: (0, n))
    in_specs = [pl.BlockSpec(memory_space=pltpu.SMEM), whole, whole]
    parts = WEIGHT_PARTS
    for part in range(parts):
        in_specs.append(
            pl.BlockSpec((depth // parts, tile), lambda n, at=chunk * parts + part: (at, n))
        )
    operands = [at, near, far] + [weight] * parts
    if before is not None:
        in_specs.append(full)
        operands.append(before)
    scratch = [pltpu.VMEM((rows, depth), BF16)]
    if last:
        out_shape = [
            jax.ShapeDtypeStruct((rows // 2, width), F32),
            jax.ShapeDtypeStruct((rows // 2, width), BF16),
        ]
        out_specs = [half, half]
        scratch.append(pltpu.VMEM((rows, tile), F32))
    else:
        out_shape = jax.ShapeDtypeStruct((rows, width), F32)
        out_specs = full
    return pl.pallas_call(
        functools.partial(
            down_kernel, rows // len(blocks), step, blocks, parts, before is None, last
        ),
        grid=(width // tile,),
        out_shape=out_shape,
        in_specs=in_specs,
        out_specs=out_specs,
        scratch_shapes=scratch,
        cost_estimate=cost(2 * rows * depth * width, 2 * depth * width + 2 * rows * depth),
        name="down_product",
        compiler_params=room(14),
    )(*operands)


def split_kernel(count, keep_ref, arrived_ref, own_ref, *refs):
    step = own_ref.shape[0]
    own_ref[...] = keep_ref[:step, :] + arrived_ref[:step, :].astype(F32)
    for far in range(1, count):
        rows = slice(far * step, (far + 1) * step)
        refs[far - 1][...] = (keep_ref[rows, :] + arrived_ref[rows, :].astype(F32)).astype(BF16)


def split(keep, arrived, count):
    rows, width = keep.shape
    step = rows // count
    piece = jax.ShapeDtypeStruct((step, width), BF16)
    return pl.pallas_call(
        functools.partial(split_kernel, count),
        grid=(1,),
        out_shape=[jax.ShapeDtypeStruct((step, width), F32)] + [piece] * (count - 1),
        in_specs=[pl.BlockSpec((rows, width), lambda n: (0, 0))] * 2,
        out_specs=[pl.BlockSpec((step, width), lambda n: (0, 0))] * count,
        cost_estimate=cost(rows * width, 8 * rows * width),
        name="split",
        compiler_params=room(8),
    )(keep, arrived)


def take_kernel(meta_ref, rows_ref, out_ref):
    step = out_ref.shape[0]
    start = pl.multiple_of(meta_ref[2] * step, step)
    out_ref[...] = rows_ref[pl.ds(start, step), :]


def take_rows(meta, rows, step):
    return pl.pallas_call(
        take_kernel,
        grid=(1,),
        out_shape=jax.ShapeDtypeStruct((step, rows.shape[1]), rows.dtype),
        in_specs=[pl.BlockSpec(memory_space=pltpu.SMEM), whole_block(rows.shape)],
        out_specs=whole_block((step, rows.shape[1])),
        cost_estimate=cost(step, 4 * rows.size),
        name="take_rows",
        compiler_params=room(4),
    )(meta, rows)


def turn_kernel(near_ref, far_ref, out_ref):
    rows = near_ref.shape[0]
    out_ref[:, :rows] = near_ref[...].T
    out_ref[:, rows:] = far_ref[...].T


def turn(near, far):
    rows, width = near.shape
    return pl.pallas_call(
        turn_kernel,
        grid=(1,),
        out_shape=jax.ShapeDtypeStruct((width, 2 * rows), near.dtype),
        in_specs=[pl.BlockSpec((rows, width), lambda n: (0, 0))] * 2,
        out_specs=pl.BlockSpec((width, 2 * rows), lambda n: (0, 0)),
        cost_estimate=cost(rows * width, 8 * rows * width),
        name="turn",
        compiler_params=room(8),
    )(near, far)


def sum_kernel(count, own_ref, *refs):
    others, before, outs = refs[: count[0]], refs[count[0] : sum(count)], refs[sum(count) :]
    total = own_ref[...].astype(F32)
    for ref in others:
        total = total + ref[...].astype(F32)
    outs[0][...] = total.astype(BF16)
    row = 0
    for ref in before:
        outs[1][row : row + ref.shape[0], :] = ref[...]
        row += ref.shape[0]
    if before:
        outs[1][row:, :] = total.astype(BF16)


def sum_rows(own, others, before=()):
    rows, width = own.shape
    out_shape = [jax.ShapeDtypeStruct(own.shape, BF16)]
    if before:
        rows += sum(value.shape[0] for value in before)
        out_shape.append(jax.ShapeDtypeStruct((rows, width), BF16))
    operands = [own, *others, *before]
    return pl.pallas_call(
        functools.partial(sum_kernel, (len(others), len(before))),
        grid=(1,),
        out_shape=out_shape,
        in_specs=[whole_block(value.shape) for value in operands],
        out_specs=[whole_block(value.shape) for value in out_shape],
        cost_estimate=cost(own.size * len(others), 12 * own.size),
        name="sum_rows",
        compiler_params=room(8),
    )(*operands)


def predict_kernel(rows_ref, proj_ref, other_ref, out_own_ref, out_other_ref):
    for weight, out in ((proj_ref, out_own_ref), (other_ref, out_other_ref)):
        out[...] = jnp.tanh(jnp.dot(rows_ref[...], weight[...], preferred_element_type=F32))


def predict(rows, proj, other):
    count, depth = rows.shape
    width = proj.shape[1]
    tile = tile_of(width, 512)
    weight = pl.BlockSpec((depth, tile), lambda n: (0, n))
    out = pl.BlockSpec((count, tile), lambda n: (0, n))
    return pl.pallas_call(
        predict_kernel,
        grid=(width // tile,),
        out_shape=[jax.ShapeDtypeStruct((count, width), F32)] * 2,
        in_specs=[pl.BlockSpec((count, depth), lambda n: (0, 0)), weight, weight],
        out_specs=[out, out],
        cost_estimate=cost(4 * count * depth * width, 4 * depth * width),
        name="predict",
        compiler_params=room(8),
    )(rows, proj, other)


def term_kernel(own_ref, other_ref, proj_ref, proj_other_ref, out_ref):
    contract = (((1,), (1,)), ((), ()))
    total = lax.dot_general(own_ref[...], proj_ref[...], contract, preferred_element_type=F32)
    total = total + lax.dot_general(
        other_ref[...], proj_other_ref[...], contract, preferred_element_type=F32
    )
    out_ref[...] = total.astype(BF16)


def student_term(own, other, proj, proj_other):
    rows, depth = own.shape
    width = proj.shape[0]
    tile = tile_of(width, 512)
    weight = pl.BlockSpec((tile, depth), lambda n: (n, 0))
    return pl.pallas_call(
        term_kernel,
        grid=(width // tile,),
        out_shape=jax.ShapeDtypeStruct((rows, width), BF16),
        in_specs=[whole_block(own.shape)] * 2 + [weight] * 2,
        out_specs=pl.BlockSpec((rows, tile), lambda n: (0, n)),
        cost_estimate=cost(4 * rows * proj.size, 4 * proj.size),
        name="student_term",
        compiler_params=room(14),
    )(own, other, proj, proj_other)


def pre_kernel(starts, meta_ref, own_ref, other_ref, *refs):
    targets, out_refs = refs[: len(starts)], refs[len(starts) :]
    half = own_ref.shape[1]
    for offset, predicted_ref in enumerate((own_ref, other_ref)):
        column = pl.multiple_of((meta_ref[2] ^ offset) * half, half)
        for start, target_ref in zip(starts, targets):
            rows = slice(start, start + target_ref.shape[0])
            predicted = predicted_ref[rows, :]
            target = target_ref[:, pl.ds(column, half)].astype(F32)
            out_refs[offset][rows, :] = (
                (predicted - target) * (1.0 - predicted * predicted)
            ).astype(BF16)


def pre_gradient(meta, own, other, targets, starts):
    out = jax.ShapeDtypeStruct(own.shape, BF16)
    whole = pl.BlockSpec(own.shape, lambda n: (0, 0))
    return pl.pallas_call(
        functools.partial(pre_kernel, tuple(starts)),
        grid=(1,),
        out_shape=[out, out],
        in_specs=[pl.BlockSpec(memory_space=pltpu.SMEM), whole, whole]
        + [pl.BlockSpec(target.shape, lambda n: (0, 0)) for target in targets],
        out_specs=[whole, whole],
        cost_estimate=cost(8 * own.size, 16 * own.size),
        name="pre_gradient",
        compiler_params=room(8),
    )(meta, own, other, *targets)


def proj_kernel(rows, step, own_ref, other_ref, *refs):
    pieces, out_ref, rhs_ref = refs[: len(rows)], refs[len(rows)], refs[len(rows) + 1]
    for places, ref in zip(rows, pieces):
        for slot, at in enumerate(places):
            rhs_ref[at * step : (at + 1) * step, :] = ref[slot * step : (slot + 1) * step, :]
    half = own_ref.shape[1]
    out_ref[...] = jnp.dot(
        own_ref[...], rhs_ref[:half, :], preferred_element_type=F32
    ) + jnp.dot(other_ref[...], rhs_ref[half:, :], preferred_element_type=F32)


def proj_product(own, other, pieces, places, step):
    rows, depth = own.shape
    width = pieces[0].shape[1]
    tile = tile_of(width, 256)
    lhs = pl.BlockSpec((rows, depth), lambda n: (0, 0))
    return pl.pallas_call(
        functools.partial(proj_kernel, places, step),
        grid=(width // tile,),
        out_shape=jax.ShapeDtypeStruct((rows, width), F32),
        in_specs=[lhs, lhs]
        + [pl.BlockSpec((piece.shape[0], tile), lambda n: (0, n)) for piece in pieces],
        out_specs=pl.BlockSpec((rows, tile), lambda n: (0, n)),
        scratch_shapes=[pltpu.VMEM((2 * depth, tile), BF16)],
        cost_estimate=cost(4 * rows * depth * width, 4 * rows * width + 4 * rows * depth),
        name="proj_product",
        compiler_params=room(8),
    )(own, other, *pieces)


def place_kernel(meta_ref, own_ref, other_ref, out_ref):
    step = own_ref.shape[0]
    for offset, ref in enumerate((own_ref, other_ref)):
        start = pl.multiple_of((meta_ref[2] ^ offset) * step, step)
        out_ref[pl.ds(start, step), :] = ref[...].astype(F32)


def place(meta, own, other):
    step, width = own.shape
    return pl.pallas_call(
        place_kernel,
        grid=(1,),
        out_shape=jax.ShapeDtypeStruct((2 * step, width), F32),
        in_specs=[pl.BlockSpec(memory_space=pltpu.SMEM)] + [whole_block(own.shape)] * 2,
        out_specs=whole_block((2 * step, width)),
        cost_estimate=cost(own.size, 12 * own.size),
        name="place",
        compiler_params=room(4),
    )(meta, own, other)


def shards(tokens, norm_gain, gate_up_weight, down_weight, student_in, student_proj):
    groups = lax.axis_size("grp")
    inner = lax.axis_size("inner")
    cores = inner // groups
    depth = inner // 2
    g = lax.axis_index("grp")
    i = lax.axis_index("inner")
    c = i & (cores - 1)
    b = i >> (cores.bit_length() - 1)
    local_rows = tokens.shape[0]
    meta = jnp.stack([i ^ (cores * g), i, c, b]).astype(jnp.int32)
    meta, tokens = lax.optimization_barrier((meta, tokens))

    places = [(x, y) for x in range(groups) for y in range(inner)]

    def move(value, target):
        pairs = []
        for x, y in places:
            to_x, to_y = target(x, y)
            pairs.append((x * inner + y, to_x * inner + to_y))
        return lax.ppermute(value, AXES, pairs)

    def over_grp(value, mask):
        return move(value, lambda x, y: (x ^ mask, y))

    def over_inner(value, mask):
        return move(value, lambda x, y: (x, y ^ mask))

    def transpose(value):
        return move(value, lambda x, y: (y // cores, x * cores + y % cores))

    bits = list(range(groups.bit_length() - 1))
    orders = (bits, bits[::-1])

    def gather(value, order):
        for bit in order[:-1]:
            arrived = over_grp(value, 1 << bit)
            value = join(value, arrived)
        return value, over_grp(value, 1 << order[-1])

    share_total = sum(ROW_SHARES)
    steps = [local_rows * share // share_total for share in ROW_SHARES]
    starts = [sum(steps[:r]) for r in range(len(steps))]

    gain = norm_gain[None, :]

    def gather_rows(r):
        own = tokens[starts[r] : starts[r] + steps[r]]
        pieces = [None] * inner
        pieces[0] = own
        for far in range(1, depth):
            pieces[2 * far] = over_inner(own, 2 * far)
        for far in range(depth):
            pieces[2 * far + 1] = over_inner(pieces[2 * far], 1)
        return pieces

    proj_other = over_inner(student_proj, 1)
    student_own = take_rows(meta, student_in, local_rows)
    near, far_rows = gather(student_own, bits)
    student_cols = turn(near, far_rows)
    student_cols_other = over_inner(student_cols, 1)
    predicted_own, predicted_other = predict(student_own, student_proj, proj_other)

    teacher_parts = []
    target_parts = []
    for r, step in enumerate(steps):
        x, squares = prepare(meta, gather_rows(r), gain)
        for bit in bits[::-1]:
            half = squares.shape[0] // 2
            squares = squares[:half] + over_grp(squares[half:], 1 << bit)
        before = None
        for chunk in range(COL_CHUNKS):
            u = r * COL_CHUNKS + chunk
            order = orders[u % 2]
            keep, send = up_product(
                x, gate_up_weight, chunk, COL_CHUNKS, scatter_list(order)
            )
            for stage, bit in enumerate(order):
                arrived = over_grp(send, 1 << bit)
                if stage < len(order) - 1:
                    keep, send = add_halves(keep, arrived)
            hidden = activate(keep, arrived, squares)
            near, far_rows = gather(hidden, order)
            last = chunk == COL_CHUNKS - 1
            before = down_product(
                meta,
                near,
                far_rows,
                down_weight,
                chunk,
                COL_CHUNKS,
                step,
                gather_list(order),
                before,
                last,
            )
        keep, send = before
        result, *sends = split(keep, over_inner(send, 1), depth)
        others = [over_inner(sends[far - 1], 2 * far) for far in range(1, depth)]
        result, *teacher_out = sum_rows(result, others, teacher_parts)
        teacher_parts.append(result)
        target_parts.append(transpose(result))

    teacher_out = teacher_out[0]
    pre_own, pre_other = pre_gradient(meta, predicted_own, predicted_other, target_parts, starts)
    pre_here = over_inner(pre_other, 1)

    total = student_term(pre_own, pre_other, student_proj, proj_other)
    for bit in range(1, inner.bit_length() - 1):
        total = sum_rows(total, [over_inner(total, 1 << bit)])[0]
    grad_student = place(meta, total, over_inner(total, 1))

    pre_pieces = []
    pre_places = []
    for half, value in enumerate((pre_own, pre_here)):
        pre_pieces.extend(gather(value, orders[half]))
        blocks = [half * groups + block for block in gather_list(orders[half])]
        pre_places.extend((blocks[: groups // 2], blocks[groups // 2 :]))
    grad_proj = proj_product(student_cols, student_cols_other, pre_pieces, pre_places, local_rows)
    return (teacher_out, grad_student, grad_proj)


def solution(mesh):
    return jax.shard_map(
        shards,
        mesh=mesh,
        in_specs=(
            P("inner", "grp"),
            P("grp"),
            P(None, "grp", "inner"),
            P("inner", "grp"),
            P("grp", None),
            P(None, "inner"),
        ),
        out_specs=(P("inner", "grp"), P("grp", None), P(None, "inner")),
        check_vma=False,
    )
```

```python
import functools

import jax
import jax.numpy as jnp
from jax import lax
from jax.experimental import pallas as pl
from jax.experimental.pallas import tpu as pltpu
from jax.sharding import PartitionSpec as P


D = 8192
AXES = ("grp", "inner")
BF16 = jnp.bfloat16
F32 = jnp.float32
ROW_SHARES = (1, 1)
COL_CHUNKS = 2
WEIGHT_PARTS = 2


def tile_of(extent, limit=1024):
    for tile in range(limit, 0, -128):
        if extent % tile == 0:
            return tile
    return extent


def cost(flops, nbytes):
    return pl.CostEstimate(flops=int(flops), bytes_accessed=int(nbytes), transcendentals=0)


def room(mebibytes):
    return pltpu.CompilerParams(vmem_limit_bytes=mebibytes << 20)


def whole_block(shape):
    return pl.BlockSpec(shape, lambda *at: (0,) * len(shape))


def scatter_list(order):
    blocks = [0]
    for bit in reversed(order):
        blocks = blocks + [block | (1 << bit) for block in blocks]
    return blocks


def gather_list(order):
    blocks = [0]
    for bit in order:
        blocks = blocks + [block ^ (1 << bit) for block in blocks]
    return blocks


def prepare_kernel(count, step, at_ref, *refs):
    pieces, gain_ref, out_ref, squares_ref = refs[:count], *refs[count:]
    gain = gain_ref[...].astype(F32)
    for offset in range(count):
        start = pl.multiple_of((at_ref[0] ^ offset) * step, step)
        values = pieces[offset][...].astype(F32)
        out_ref[pl.ds(start, step), :] = (values * gain).astype(BF16)
        total = jnp.sum(values * values, axis=1, keepdims=True)
        squares_ref[pl.ds(start, step), :] = jnp.broadcast_to(total, (step, 128))


def prepare(at, pieces, gain):
    count = len(pieces)
    step, width = pieces[0].shape
    return pl.pallas_call(
        functools.partial(prepare_kernel, count, step),
        grid=(1,),
        out_shape=[
            jax.ShapeDtypeStruct((count * step, width), BF16),
            jax.ShapeDtypeStruct((count * step, 128), F32),
        ],
        in_specs=[pl.BlockSpec(memory_space=pltpu.SMEM)]
        + [whole_block((step, width))] * count
        + [whole_block(gain.shape)],
        out_specs=[whole_block((count * step, width)), whole_block((count * step, 128))],
        cost_estimate=cost(3 * count * step * width, 4 * count * step * width),
        name="prepare",
        compiler_params=room(8),
    )(at, *pieces, gain)


def up_kernel(block, blocks, start, tile, x_ref, source_ref, keep_ref, send_ref, w_ref, sems):
    tiles = w_ref.shape[2] // tile
    half = len(blocks) // 2

    def copy(k, n):
        column = pl.multiple_of(n * tile, tile)
        return pltpu.make_async_copy(
            source_ref.at[k, :, pl.ds(start + column, tile)],
            w_ref.at[k, :, pl.ds(column, tile)],
            sems.at[k, n],
        )

    for k in range(2):
        for n in range(tiles):
            copy(k, n).start()
    for k in range(2):

        @pl.loop(0, tiles)
        def _(n):
            copy(k, n).wait()
            columns = pl.ds(pl.multiple_of(n * tile, tile), tile)
            total = jnp.dot(x_ref[...], w_ref[k, :, columns], preferred_element_type=F32)
            for slot, at in enumerate(blocks):
                ref = send_ref if slot >= half else keep_ref
                row = (slot % half) * block
                ref[k, row : row + block, columns] = total[
                    at * block : (at + 1) * block, :
                ].astype(BF16)


def up_product(x, weight, chunk, chunks, blocks):
    rows, depth = x.shape
    width = weight.shape[2] // chunks
    tile = tile_of(width, 256)
    half = jax.ShapeDtypeStruct((2, rows // 2, width), BF16)
    return pl.pallas_call(
        functools.partial(up_kernel, rows // len(blocks), blocks, chunk * width, tile),
        grid=(1,),
        out_shape=[half] * 2,
        in_specs=[whole_block(x.shape), pl.BlockSpec(memory_space=pltpu.HBM)],
        out_specs=[whole_block(half.shape)] * 2,
        scratch_shapes=[
            pltpu.VMEM((2, depth, width), BF16),
            pltpu.SemaphoreType.DMA((2, width // tile)),
        ],
        cost_estimate=cost(4 * rows * depth * width, 4 * depth * width + 2 * rows * depth),
        name="up_product",
        compiler_params=room(32),
    )(x, weight)


def add_kernel(keep_ref, arrived_ref, kept_ref, send_ref):
    rows = kept_ref.shape[0]
    total = keep_ref[...].astype(F32) + arrived_ref[...].astype(F32)
    kept_ref[...] = total[:rows]
    send_ref[...] = total[rows:].astype(BF16)


def add_halves(keep, arrived):
    _, rows, width = keep.shape
    whole = pl.BlockSpec((None, rows, width), lambda k: (k, 0, 0))
    half = pl.BlockSpec((None, rows // 2, width), lambda k: (k, 0, 0))
    return pl.pallas_call(
        add_kernel,
        grid=(2,),
        out_shape=[
            jax.ShapeDtypeStruct((2, rows // 2, width), F32),
            jax.ShapeDtypeStruct((2, rows // 2, width), BF16),
        ],
        in_specs=[whole] * 2,
        out_specs=[half] * 2,
        cost_estimate=cost(2 * rows * width, 14 * rows * width),
        name="add_halves",
        compiler_params=room(8),
    )(keep, arrived)


def activate_kernel(depth, keep_ref, arrived_ref, squares_ref, out_ref):
    inverse = lax.rsqrt(squares_ref[:, :1] / depth + 1e-05)
    gate = (keep_ref[0].astype(F32) + arrived_ref[0].astype(F32)) * inverse
    up = (keep_ref[1].astype(F32) + arrived_ref[1].astype(F32)) * inverse
    out_ref[...] = (jax.nn.silu(gate) * up).astype(BF16)


def activate(keep, arrived, squares):
    _, rows, width = keep.shape
    tile = tile_of(width)
    both = pl.BlockSpec((2, rows, tile), lambda n: (0, 0, n))
    return pl.pallas_call(
        functools.partial(activate_kernel, D),
        grid=(width // tile,),
        out_shape=jax.ShapeDtypeStruct((rows, width), BF16),
        in_specs=[both, both, whole_block(squares.shape)],
        out_specs=pl.BlockSpec((rows, tile), lambda n: (0, n)),
        cost_estimate=cost(10 * rows * width, 14 * rows * width),
        name="activate",
        compiler_params=room(8),
    )(keep, arrived, squares)


def join_kernel(near_ref, far_ref, out_ref):
    rows = near_ref.shape[0]
    out_ref[:rows, :] = near_ref[...]
    out_ref[rows:, :] = far_ref[...]


def join(near, far):
    rows, width = near.shape
    return pl.pallas_call(
        join_kernel,
        grid=(1,),
        out_shape=jax.ShapeDtypeStruct((2 * rows, width), near.dtype),
        in_specs=[pl.BlockSpec((rows, width), lambda n: (0, 0))] * 2,
        out_specs=pl.BlockSpec((2 * rows, width), lambda n: (0, 0)),
        cost_estimate=cost(rows * width, 8 * rows * width),
        name="join",
        compiler_params=room(8),
    )(near, far)


def down_kernel(block, step, lists, parts, first, last, at_ref, *refs):
    pieces, refs = refs[: 2 * len(lists)], refs[2 * len(lists) :]
    w_refs, refs = refs[:parts], refs[parts:]
    if not first:
        before_ref, refs = refs[0], refs[1:]
    if last:
        keep_ref, send_ref, lhs_ref, total_ref = refs
    else:
        total_ref, lhs_ref = refs

    @pl.when(pl.program_id(0) == 0)
    def _():
        for chunk, blocks in enumerate(lists):
            half = len(blocks) // 2
            for slot, at in enumerate(blocks):
                ref = pieces[2 * chunk + slot // half]
                source = (slot % half) * block
                column = chunk * ref.shape[1]
                lhs_ref[at * block : (at + 1) * block, column : column + ref.shape[1]] = ref[
                    source : source + block, :
                ]

    part = w_refs[0].shape[0]
    total = 0.0
    for at, w_ref in enumerate(w_refs):
        total += jnp.dot(
            lhs_ref[:, at * part : (at + 1) * part], w_ref[...], preferred_element_type=F32
        )
    if not first:
        total = total + before_ref[...]
    total_ref[...] = total
    if last:
        for slot in range(total.shape[0] // step):
            start = pl.multiple_of((at_ref[0] ^ slot) * step, step)
            rows = total_ref[pl.ds(start, step), :]
            row = (slot // 2) * step
            if slot % 2 == 0:
                keep_ref[row : row + step, :] = rows
            else:
                send_ref[row : row + step, :] = rows.astype(BF16)


def down_product(at, pieces, weight, chunk, chunks, step, lists, before, last):
    rows = 2 * pieces[0].shape[0]
    depth = len(lists) * (weight.shape[0] // chunks)
    width = weight.shape[1]
    tile = tile_of(width, 1024 // len(lists))
    full = pl.BlockSpec((rows, tile), lambda n: (0, n))
    half = pl.BlockSpec((rows // 2, tile), lambda n: (0, n))
    in_specs = [pl.BlockSpec(memory_space=pltpu.SMEM)]
    in_specs += [whole_block(piece.shape) for piece in pieces]
    parts = WEIGHT_PARTS * len(lists)
    start = chunk * WEIGHT_PARTS
    for part in range(parts):
        in_specs.append(pl.BlockSpec((depth // parts, tile), lambda n, at=start + part: (at, n)))
    operands = [at, *pieces] + [weight] * parts
    if before is not None:
        in_specs.append(full)
        operands.append(before)
    scratch = [pltpu.VMEM((rows, depth), BF16)]
    if last:
        out_shape = [
            jax.ShapeDtypeStruct((rows // 2, width), F32),
            jax.ShapeDtypeStruct((rows // 2, width), BF16),
        ]
        out_specs = [half, half]
        scratch.append(pltpu.VMEM((rows, tile), F32))
    else:
        out_shape = jax.ShapeDtypeStruct((rows, width), F32)
        out_specs = full
    return pl.pallas_call(
        functools.partial(
            down_kernel, rows // len(lists[0]), step, lists, parts, before is None, last
        ),
        grid=(width // tile,),
        out_shape=out_shape,
        in_specs=in_specs,
        out_specs=out_specs,
        scratch_shapes=scratch,
        cost_estimate=cost(2 * rows * depth * width, 2 * depth * width + 2 * rows * depth),
        name="down_product",
        compiler_params=room(24),
    )(*operands)


def split_kernel(count, keep_ref, arrived_ref, own_ref, *refs):
    step = own_ref.shape[0]
    own_ref[...] = keep_ref[:step, :] + arrived_ref[:step, :].astype(F32)
    for far in range(1, count):
        rows = slice(far * step, (far + 1) * step)
        refs[far - 1][...] = (keep_ref[rows, :] + arrived_ref[rows, :].astype(F32)).astype(BF16)


def split(keep, arrived, count):
    rows, width = keep.shape
    step = rows // count
    piece = jax.ShapeDtypeStruct((step, width), BF16)
    return pl.pallas_call(
        functools.partial(split_kernel, count),
        grid=(1,),
        out_shape=[jax.ShapeDtypeStruct((step, width), F32)] + [piece] * (count - 1),
        in_specs=[pl.BlockSpec((rows, width), lambda n: (0, 0))] * 2,
        out_specs=[pl.BlockSpec((step, width), lambda n: (0, 0))] * count,
        cost_estimate=cost(rows * width, 8 * rows * width),
        name="split",
        compiler_params=room(8),
    )(keep, arrived)


def take_kernel(meta_ref, rows_ref, out_ref):
    step = out_ref.shape[0]
    start = pl.multiple_of(meta_ref[2] * step, step)
    out_ref[...] = rows_ref[pl.ds(start, step), :]


def take_rows(meta, rows, step):
    return pl.pallas_call(
        take_kernel,
        grid=(1,),
        out_shape=jax.ShapeDtypeStruct((step, rows.shape[1]), rows.dtype),
        in_specs=[pl.BlockSpec(memory_space=pltpu.SMEM), whole_block(rows.shape)],
        out_specs=whole_block((step, rows.shape[1])),
        cost_estimate=cost(step, 4 * rows.size),
        name="take_rows",
        compiler_params=room(4),
    )(meta, rows)


def turn_kernel(near_ref, far_ref, out_ref):
    rows = near_ref.shape[0]
    out_ref[:, :rows] = near_ref[...].T
    out_ref[:, rows:] = far_ref[...].T


def turn(near, far):
    rows, width = near.shape
    return pl.pallas_call(
        turn_kernel,
        grid=(1,),
        out_shape=jax.ShapeDtypeStruct((width, 2 * rows), near.dtype),
        in_specs=[pl.BlockSpec((rows, width), lambda n: (0, 0))] * 2,
        out_specs=pl.BlockSpec((width, 2 * rows), lambda n: (0, 0)),
        cost_estimate=cost(rows * width, 8 * rows * width),
        name="turn",
        compiler_params=room(8),
    )(near, far)


def sum_kernel(count, own_ref, *refs):
    others, before, outs = refs[: count[0]], refs[count[0] : sum(count)], refs[sum(count) :]
    total = own_ref[...].astype(F32)
    for ref in others:
        total = total + ref[...].astype(F32)
    outs[0][...] = total.astype(BF16)
    row = 0
    for ref in before:
        outs[1][row : row + ref.shape[0], :] = ref[...]
        row += ref.shape[0]
    if before:
        outs[1][row:, :] = total.astype(BF16)


def sum_rows(own, others, before=()):
    rows, width = own.shape
    out_shape = [jax.ShapeDtypeStruct(own.shape, BF16)]
    if before:
        rows += sum(value.shape[0] for value in before)
        out_shape.append(jax.ShapeDtypeStruct((rows, width), BF16))
    operands = [own, *others, *before]
    return pl.pallas_call(
        functools.partial(sum_kernel, (len(others), len(before))),
        grid=(1,),
        out_shape=out_shape,
        in_specs=[whole_block(value.shape) for value in operands],
        out_specs=[whole_block(value.shape) for value in out_shape],
        cost_estimate=cost(own.size * len(others), 12 * own.size),
        name="sum_rows",
        compiler_params=room(8),
    )(*operands)


def predict_kernel(rows_ref, proj_ref, other_ref, out_own_ref, out_other_ref):
    for weight, out in ((proj_ref, out_own_ref), (other_ref, out_other_ref)):
        out[...] = jnp.tanh(jnp.dot(rows_ref[...], weight[...], preferred_element_type=F32))


def predict(rows, proj, other):
    count, depth = rows.shape
    width = proj.shape[1]
    tile = tile_of(width, 512)
    weight = pl.BlockSpec((depth, tile), lambda n: (0, n))
    out = pl.BlockSpec((count, tile), lambda n: (0, n))
    return pl.pallas_call(
        predict_kernel,
        grid=(width // tile,),
        out_shape=[jax.ShapeDtypeStruct((count, width), F32)] * 2,
        in_specs=[pl.BlockSpec((count, depth), lambda n: (0, 0)), weight, weight],
        out_specs=[out, out],
        cost_estimate=cost(4 * count * depth * width, 4 * depth * width),
        name="predict",
        compiler_params=room(8),
    )(rows, proj, other)


def term_kernel(own_ref, other_ref, proj_ref, proj_other_ref, out_ref):
    contract = (((1,), (1,)), ((), ()))
    total = lax.dot_general(own_ref[...], proj_ref[...], contract, preferred_element_type=F32)
    total = total + lax.dot_general(
        other_ref[...], proj_other_ref[...], contract, preferred_element_type=F32
    )
    out_ref[...] = total.astype(BF16)


def student_term(own, other, proj, proj_other):
    rows, depth = own.shape
    width = proj.shape[0]
    tile = tile_of(width, 512)
    weight = pl.BlockSpec((tile, depth), lambda n: (n, 0))
    return pl.pallas_call(
        term_kernel,
        grid=(width // tile,),
        out_shape=jax.ShapeDtypeStruct((rows, width), BF16),
        in_specs=[whole_block(own.shape)] * 2 + [weight] * 2,
        out_specs=pl.BlockSpec((rows, tile), lambda n: (0, n)),
        cost_estimate=cost(4 * rows * proj.size, 4 * proj.size),
        name="student_term",
        compiler_params=room(14),
    )(own, other, proj, proj_other)


def pre_kernel(starts, meta_ref, own_ref, other_ref, *refs):
    targets, out_refs = refs[: len(starts)], refs[len(starts) :]
    half = own_ref.shape[1]
    for offset, predicted_ref in enumerate((own_ref, other_ref)):
        column = pl.multiple_of((meta_ref[2] ^ offset) * half, half)
        for start, target_ref in zip(starts, targets):
            rows = slice(start, start + target_ref.shape[0])
            predicted = predicted_ref[rows, :]
            target = target_ref[:, pl.ds(column, half)].astype(F32)
            out_refs[offset][rows, :] = (
                (predicted - target) * (1.0 - predicted * predicted)
            ).astype(BF16)


def pre_gradient(meta, own, other, targets, starts):
    out = jax.ShapeDtypeStruct(own.shape, BF16)
    whole = pl.BlockSpec(own.shape, lambda n: (0, 0))
    return pl.pallas_call(
        functools.partial(pre_kernel, tuple(starts)),
        grid=(1,),
        out_shape=[out, out],
        in_specs=[pl.BlockSpec(memory_space=pltpu.SMEM), whole, whole]
        + [pl.BlockSpec(target.shape, lambda n: (0, 0)) for target in targets],
        out_specs=[whole, whole],
        cost_estimate=cost(8 * own.size, 16 * own.size),
        name="pre_gradient",
        compiler_params=room(8),
    )(meta, own, other, *targets)


def proj_kernel(rows, step, own_ref, other_ref, *refs):
    pieces, out_ref, rhs_ref = refs[: len(rows)], refs[len(rows)], refs[len(rows) + 1]
    for places, ref in zip(rows, pieces):
        for slot, at in enumerate(places):
            rhs_ref[at * step : (at + 1) * step, :] = ref[slot * step : (slot + 1) * step, :]
    half = own_ref.shape[1]
    out_ref[...] = jnp.dot(
        own_ref[...], rhs_ref[:half, :], preferred_element_type=F32
    ) + jnp.dot(other_ref[...], rhs_ref[half:, :], preferred_element_type=F32)


def proj_product(own, other, pieces, places, step):
    rows, depth = own.shape
    width = pieces[0].shape[1]
    tile = tile_of(width, 256)
    lhs = pl.BlockSpec((rows, depth), lambda n: (0, 0))
    return pl.pallas_call(
        functools.partial(proj_kernel, places, step),
        grid=(width // tile,),
        out_shape=jax.ShapeDtypeStruct((rows, width), F32),
        in_specs=[lhs, lhs]
        + [pl.BlockSpec((piece.shape[0], tile), lambda n: (0, n)) for piece in pieces],
        out_specs=pl.BlockSpec((rows, tile), lambda n: (0, n)),
        scratch_shapes=[pltpu.VMEM((2 * depth, tile), BF16)],
        cost_estimate=cost(4 * rows * depth * width, 4 * rows * width + 4 * rows * depth),
        name="proj_product",
        compiler_params=room(8),
    )(own, other, *pieces)


def place_kernel(meta_ref, own_ref, other_ref, out_ref):
    step = own_ref.shape[0]
    for offset, ref in enumerate((own_ref, other_ref)):
        start = pl.multiple_of((meta_ref[2] ^ offset) * step, step)
        out_ref[pl.ds(start, step), :] = ref[...].astype(F32)


def place(meta, own, other):
    step, width = own.shape
    return pl.pallas_call(
        place_kernel,
        grid=(1,),
        out_shape=jax.ShapeDtypeStruct((2 * step, width), F32),
        in_specs=[pl.BlockSpec(memory_space=pltpu.SMEM)] + [whole_block(own.shape)] * 2,
        out_specs=whole_block((2 * step, width)),
        cost_estimate=cost(own.size, 12 * own.size),
        name="place",
        compiler_params=room(4),
    )(meta, own, other)


def shards(tokens, norm_gain, gate_up_weight, down_weight, student_in, student_proj):
    groups = lax.axis_size("grp")
    inner = lax.axis_size("inner")
    cores = inner // groups
    depth = inner // 2
    g = lax.axis_index("grp")
    i = lax.axis_index("inner")
    c = i & (cores - 1)
    b = i >> (cores.bit_length() - 1)
    local_rows = tokens.shape[0]
    meta = jnp.stack([i ^ (cores * g), i, c, b]).astype(jnp.int32)
    meta, tokens = lax.optimization_barrier((meta, tokens))

    places = [(x, y) for x in range(groups) for y in range(inner)]

    def move(value, target):
        pairs = []
        for x, y in places:
            to_x, to_y = target(x, y)
            pairs.append((x * inner + y, to_x * inner + to_y))
        return lax.ppermute(value, AXES, pairs)

    def over_grp(value, mask):
        return move(value, lambda x, y: (x ^ mask, y))

    def over_inner(value, mask):
        return move(value, lambda x, y: (x, y ^ mask))

    def transpose(value):
        return move(value, lambda x, y: (y // cores, x * cores + y % cores))

    bits = list(range(groups.bit_length() - 1))
    orders = (bits, bits[::-1])

    def gather(value, order):
        for bit in order[:-1]:
            arrived = over_grp(value, 1 << bit)
            value = join(value, arrived)
        return value, over_grp(value, 1 << order[-1])

    share_total = sum(ROW_SHARES)
    steps = [local_rows * share // share_total for share in ROW_SHARES]
    starts = [sum(steps[:r]) for r in range(len(steps))]

    gain = norm_gain[None, :]

    def gather_rows(r):
        own = tokens[starts[r] : starts[r] + steps[r]]
        pieces = [None] * inner
        pieces[0] = own
        for far in range(1, depth):
            pieces[2 * far] = over_inner(own, 2 * far)
        for far in range(depth):
            pieces[2 * far + 1] = over_inner(pieces[2 * far], 1)
        return pieces

    proj_other = over_inner(student_proj, 1)
    student_own = take_rows(meta, student_in, local_rows)
    near, far_rows = gather(student_own, bits)
    student_cols = turn(near, far_rows)
    student_cols_other = over_inner(student_cols, 1)
    predicted_own, predicted_other = predict(student_own, student_proj, proj_other)

    teacher_parts = []
    target_parts = []
    for r, step in enumerate(steps):
        x, squares = prepare(meta, gather_rows(r), gain)
        squares = squares.reshape(groups, squares.shape[0] // groups, 128)
        for bit in bits if r else bits[::-1]:
            half = squares.shape[0] // 2
            keep, send = squares[:half], squares[half:]
            if r:
                keep, send = squares[::2], squares[1::2]
            squares = keep + over_grp(send, 1 << bit)
        squares = squares[0]
        before = None
        pieces, lists = [], []
        for chunk in range(COL_CHUNKS):
            u = r * COL_CHUNKS + chunk
            order = orders[u % 2]
            keep, send = up_product(
                x, gate_up_weight, chunk, COL_CHUNKS, scatter_list(order)
            )
            for stage, bit in enumerate(order):
                arrived = over_grp(send, 1 << bit)
                if stage < len(order) - 1:
                    keep, send = add_halves(keep, arrived)
            hidden = activate(keep, arrived, squares)
            pieces.extend(gather(hidden, order))
            lists.append(gather_list(order))
            last = chunk == COL_CHUNKS - 1
            if last or r < len(steps) - 1:
                before = down_product(
                    meta,
                    pieces,
                    down_weight,
                    chunk + 1 - len(lists),
                    COL_CHUNKS,
                    step,
                    lists,
                    before,
                    last,
                )
                pieces, lists = [], []
        keep, send = before
        result, *sends = split(keep, over_inner(send, 1), depth)
        others = [over_inner(sends[far - 1], 2 * far) for far in range(1, depth)]
        result, *teacher_out = sum_rows(result, others, teacher_parts)
        teacher_parts.append(result)
        target_parts.append(transpose(result))

    teacher_out = teacher_out[0]
    pre_own, pre_other = pre_gradient(meta, predicted_own, predicted_other, target_parts, starts)
    pre_here = over_inner(pre_other, 1)

    total = student_term(pre_own, pre_other, student_proj, proj_other)
    for bit in range(1, inner.bit_length() - 1):
        total = sum_rows(total, [over_inner(total, 1 << bit)])[0]
    grad_student = place(meta, total, over_inner(total, 1))

    pre_pieces = []
    pre_places = []
    for half, value in enumerate((pre_own, pre_here)):
        pre_pieces.extend(gather(value, orders[half]))
        blocks = [half * groups + block for block in gather_list(orders[half])]
        pre_places.extend((blocks[: groups // 2], blocks[groups // 2 :]))
    grad_proj = proj_product(student_cols, student_cols_other, pre_pieces, pre_places, local_rows)
    return (teacher_out, grad_student, grad_proj)


def solution(mesh):
    return jax.shard_map(
        shards,
        mesh=mesh,
        in_specs=(
            P("inner", "grp"),
            P("grp"),
            P(None, "grp", "inner"),
            P("inner", "grp"),
            P("grp", None),
            P(None, "inner"),
        ),
        out_specs=(P("inner", "grp"), P("grp", None), P(None, "inner")),
        check_vma=False,
    )
```
